128 devices in a mesh: cond: 16 (over z_hi, x, core), ty: 4 (over y), tx: 2 (over z_lo).
Axes of the slice: x: 4, y: 4, z: 4 (z_hi: 2, z_lo: 2; z = z_hi * 2 + z_lo), core: 2. Of those that a mesh axis runs over, the one named last changes fastest.
Arguments:
- bed: float32 [1024, 2048], P('ty', 'tx'), may hold values from -4 to 4
- land_mask: int32 [1024, 2048], P('ty', 'tx'), may hold values 0 or 1
- cell_class: int32 [1024, 2048], P('ty', 'tx'), may hold values from 0 to 2
- weights: int32 [16], replicated, may hold values from 1 to 8
- cond_params: float32 [16, 4], P('cond'), may hold values from 0.25 to 2
- wave_stress: float32 [16, 2, 1024, 2048], P('cond', None, 'ty', 'tx'), may hold values from -0.6 to 0.6
- hydro_state: float32 [16, 3, 1024, 2048], P('cond', None, 'ty', 'tx'), may hold values from -1.8 to 1.8
Outputs:
- bed_next: float32 [1024, 2048], P('ty', 'tx')
- bed_change: float32 [1024, 2048], P('ty', 'tx')
- hydro_next: float32 [16, 3, 1024, 2048], P('cond', None, 'ty', 'tx')
The draws below stay inside these ranges and needn't reach their ends.
All inputs are finite; a program needn't handle non-finite values. No bound on the sum of `land_mask` on one device may be relied on, other than what follows from the above.
Results may differ from the reference program's by a relative error of at most 0.00002.
Values sent between devices are 32-bit elements; how exact they have to be, the bound alone decides.
A program may use at most 128 MiB of HBM per device.

```python
import math
import jax
import jax.numpy as jnp

STEPS = 3
CONDS = 16
NR = 1024
NC = 2048


def place_ends(result, own_key, least, high):
    place = [jax.random.randint(jax.random.fold_in(own_key, axis), (), 0, length) for axis, length in enumerate(result.shape)]
    main_axis = result.shape.index(max(result.shape))
    neighbour = place[:main_axis] + [(place[main_axis] + 1) % result.shape[main_axis]] + place[main_axis + 1:]
    return result.at[tuple(place)].set(least).at[tuple(neighbour)].set(high)


def block_levels(key, shape, shards, low, top_value):
    factor_of, own = 1.0, jax.random.fold_in(key, 6)
    for axis_at, parts in shards:
        steps = jnp.exp(jax.random.uniform(jax.random.fold_in(own, axis_at), (parts,), jnp.float32, low / len(shards), top_value / len(shards)))
        factor_of = factor_of * jnp.repeat(steps, shape[axis_at] // parts).reshape([-1 if axis == axis_at else 1 for axis in range(len(shape))])
    return factor_of


def bell_draw(stream_key, dims, width, reach, cuts=(), dtype=jnp.bfloat16):
    gain = block_levels(stream_key, dims, cuts, -0.22, 0.18) if cuts else 1.0
    drawn = jax.random.normal(stream_key, dims, jnp.float32) * width * gain
    return jnp.minimum(jnp.maximum(drawn, -reach), reach).astype(dtype)


def setup_inputs(seed: int = 0) -> dict:
    key_of = jax.random.split(jax.random.key(seed), 8)
    return {
        "bed": bell_draw(key_of[0], (NR, NC), 1.0, 4.0, ((0, 4), (1, 2)), jnp.float32),
        "land_mask": place_ends((jax.random.randint(key_of[1], (NR, NC), 0, 4) < 3).astype(jnp.int32), jax.random.fold_in(key_of[1], 1), 0, 1),
        "cell_class": place_ends(jax.random.randint(key_of[2], (NR, NC), 0, 3), jax.random.fold_in(key_of[2], 1), 0, 2).astype(jnp.int32),
        "weights": place_ends(jax.random.randint(key_of[3], (CONDS,), 1, 9), jax.random.fold_in(key_of[3], 1), 1, 8).astype(jnp.int32),
        "cond_params": jnp.clip(jnp.exp(math.log(2.0) - 2.0794415 * jax.random.uniform(key_of[4], (CONDS, 4), jnp.float32) ** block_levels(key_of[4], (CONDS, 4), ((0, 16),), -0.2, 0.2)), 0.25, 2.0),
        "wave_stress": bell_draw(key_of[5], (CONDS, 2, NR, NC), 0.1, 0.6, ((0, 16), (2, 4), (3, 2)), jnp.float32),
        "hydro_state": bell_draw(key_of[6], (CONDS, 3, NR, NC), 0.3, 1.8, ((0, 16), (2, 4), (3, 2)), jnp.float32),
    }


def east(x):
    return jnp.concatenate([x[:, 1:], jnp.zeros_like(x[:, :1])], axis=1)

def west(x):
    return jnp.concatenate([jnp.zeros_like(x[:, :1]), x[:, :-1]], axis=1)

def south(x):
    return jnp.concatenate([x[1:, :], jnp.zeros_like(x[:1, :])], axis=0)

def north(x):
    return jnp.concatenate([jnp.zeros_like(x[:1, :]), x[:-1, :]], axis=0)

def reference(bed, land_mask, cell_class, weights, cond_params, wave_stress, hydro_state):
    wet = land_mask.astype(jnp.float32)
    depth = wet * (1.0 + 0.5 * jnp.tanh(-bed))
    relax = 0.5 * depth * (cell_class == 1).astype(jnp.float32)
    inflow = depth * (cell_class == 2).astype(jnp.float32)
    face_c = jnp.sqrt(depth * east(depth))
    face_r = jnp.sqrt(depth * south(depth))
    wet_c = face_c / (face_c + 0.1)
    wet_r = face_r / (face_r + 0.1)
    wsum = jnp.sum(weights).astype(jnp.float32)
    total = jnp.zeros(bed.shape, jnp.float32)
    states = []
    for cond in range(CONDS):
        tide = cond_params[cond, 0] - 1.0
        fric = 0.2 * cond_params[cond, 1]
        coef = cond_params[cond, 2]
        flow_in = 0.3 * cond_params[cond, 3]
        level = hydro_state[cond, 0]
        vel_c = hydro_state[cond, 1]
        vel_r = hydro_state[cond, 2]
        stress_c = wave_stress[cond, 0]
        stress_r = wave_stress[cond, 1]
        change = jnp.zeros(bed.shape, jnp.float32)
        for step in range(STEPS):
            vel_c = ((1.0 - fric) * vel_c - 0.3 * (east(level) - level) + stress_c) * wet_c
            vel_r = ((1.0 - fric) * vel_r - 0.3 * (south(level) - level) + stress_r) * wet_r
            flux_c = face_c * vel_c
            flux_r = face_r * vel_r
            level = level - (flux_c - west(flux_c) + flux_r - north(flux_r)) + relax * (tide - level) + flow_in * inflow
            load_c = coef * wet_c * vel_c * jnp.abs(vel_c)
            load_r = coef * wet_r * vel_r * jnp.abs(vel_r)
            change = change - 4.0 * (load_c - west(load_c) + load_r - north(load_r))
        states.append(jnp.stack([level, vel_c, vel_r]))
        total = total + weights[cond].astype(jnp.float32) / wsum * change
    height = bed + total
    col_ids = jnp.arange(NC)[None, :]
    row_ids = jnp.arange(NR)[:, None]
    inside_c = (col_ids < NC - 1).astype(jnp.float32)
    inside_r = (row_ids < NR - 1).astype(jnp.float32)
    slope_c = (east(height) - height) * inside_c
    slope_r = (south(height) - height) * inside_r
    spill_c = 0.25 * (slope_c - jnp.clip(slope_c, -1.0, 1.0))
    spill_r = 0.25 * (slope_r - jnp.clip(slope_r, -1.0, 1.0))
    bed_next = height + spill_c - west(spill_c) + spill_r - north(spill_r)
    return (bed_next, total, jnp.stack(states))
```

```python
import functools

import jax
import jax.numpy as jnp
from jax import lax
from jax.experimental import pallas as pl
from jax.experimental.pallas import tpu as pltpu
from jax.sharding import PartitionSpec as P

MESH = pl.DeviceIdType.MESH
F32 = jnp.float32
LANE = 128
EDGE = 8
HALO = 4
R = 16
NX = 4
CHUNKS = (5, 4, 4, 4)


def kernel(
    rows,
    cols,
    chunks,
    bed_h,
    mask_h,
    cls_h,
    wts,
    par,
    stress_h,
    hydro_h,
    bn_h,
    bc_h,
    hy_h,
    E,
    U,
    V,
    SX,
    SY,
    BED,
    MASK,
    CLS,
    D,
    WC,
    WR,
    FC,
    FR,
    A,
    B,
    QC,
    QR,
    T,
    M,
    BN,
    CF,
    CQ,
    EDF,
    EDI,
    PS,
    RSTRIP,
    CR,
    PP,
    RAL,
    RAR,
    RBL,
    RBR,
    RCL,
    RCR,
    C1,
    C2,
    S,
    RZ,
    in_sem,
    edge_sem,
    halo_send,
    halo_recv,
    strip_send,
    strip_recv,
    ring_send,
    ring_recv,
    out_sem,
):
    nrow = rows + 2 * EDGE
    width = cols + LANE
    nblk = nrow // R
    c = lax.axis_index("cond")
    ty = lax.axis_index("ty")
    tx = lax.axis_index("tx")
    nty = lax.axis_size("ty")
    ntx = lax.axis_size("tx")
    core = c % 2
    x = (c // 2) % NX
    zh = c // (2 * NX)
    up = (ty + nty - 1) % nty
    down = (ty + 1) % nty
    side = 1 - tx
    xr = (x + 1) % NX
    xl = (x + NX - 1) % NX
    xf = (x + 2) % NX

    def cond_of(z, xx, k):
        return (z * NX + xx) * 2 + k

    sibling = (cond_of(zh, x, 1 - core), ty, tx)
    right = (cond_of(zh, xr, core), ty, tx)
    left = (cond_of(zh, xl, core), ty, tx)
    zpeer = (cond_of(1 - zh, x, core), ty, tx)
    above = (c, up, tx)
    below = (c, down, tx)
    beside = (c, ty, side)
    diag_up = (c, up, side)
    diag_down = (c, down, side)

    fields = (E, U, V, SX, SY, BED, MASK, CLS)
    sources = (
        hydro_h.at[0, 0],
        hydro_h.at[0, 1],
        hydro_h.at[0, 2],
        stress_h.at[0, 0],
        stress_h.at[0, 1],
        bed_h,
        mask_h,
        cls_h,
    )
    edge_at = pl.multiple_of((1 - tx) * (cols - LANE), LANE)
    edges = [EDF.at[i] for i in range(6)] + [EDI.at[i] for i in range(2)]

    edge_copies = [
        pltpu.make_async_copy(src.at[:, pl.ds(edge_at, LANE)], dst, edge_sem.at[i])
        for i, (src, dst) in enumerate(zip(sources, edges))
    ]
    for copy in edge_copies:
        copy.start()
    in_copies = [
        pltpu.make_async_copy(src, dst.at[EDGE : EDGE + rows, 0:cols], in_sem.at[i])
        for i, (src, dst) in enumerate(zip(sources, fields))
    ]
    for i in (5, 6, 0, 1, 2, 3, 4, 7):
        in_copies[i].start()

    pad = EDGE - HALO
    for field in fields:
        field[0:pad, 0:cols] = jnp.zeros((pad, cols), field.dtype)
        field[nrow - pad : nrow, 0:cols] = jnp.zeros((pad, cols), field.dtype)
    E[nrow : nrow + 8, :] = jnp.zeros((8, width), F32)
    D[nrow : nrow + 8, :] = jnp.zeros((8, width), F32)
    M[0:EDGE, cols:width] = jnp.zeros((EDGE, LANE), F32)
    M[nrow - EDGE : nrow, cols:width] = jnp.zeros((EDGE, LANE), F32)

    barrier = pltpu.get_barrier_semaphore()
    peers = (sibling, right, left, zpeer, above, below, beside, diag_up, diag_down)
    for peer in peers:
        pl.semaphore_signal(barrier, inc=1, device_id=peer, device_id_type=MESH)
    pl.semaphore_wait(barrier, len(peers))

    def remote(src, dst, send, recv, peer):
        copy = pltpu.make_async_remote_copy(
            src_ref=src, dst_ref=dst, send_sem=send, recv_sem=recv, device_id=peer, device_id_type=MESH
        )
        copy.start()
        return copy

    halo_copies = []
    for i, (src, dst) in enumerate(zip(sources, fields)):
        halo_copies.append(
            remote(
                src.at[rows - HALO : rows, :],
                dst.at[EDGE - HALO : EDGE, 0:cols],
                halo_send.at[0, i],
                halo_recv.at[0, i],
                below,
            )
        )
        halo_copies.append(
            remote(
                src.at[0:HALO, :],
                dst.at[EDGE + rows : EDGE + rows + HALO, 0:cols],
                halo_send.at[1, i],
                halo_recv.at[1, i],
                above,
            )
        )

    lanes = lax.broadcasted_iota(jnp.int32, (R, LANE), 1)
    for copy in edge_copies:
        copy.wait()

    def pack(i, carry):
        r = pl.multiple_of(i * R, R)
        strip = jnp.zeros((R, LANE), F32)
        for k in range(8):
            cells = edges[k][pl.ds(r, R), :].astype(F32)
            cells = pltpu.roll(cells, HALO * k + HALO * (1 - tx), 1)
            strip = jnp.where((lanes >= HALO * k) & (lanes < HALO * (k + 1)), cells, strip)
        PS[pl.ds(r, R), :] = strip
        return carry

    lax.fori_loop(0, rows // R, pack, 0)
    strip_copies = [
        remote(PS, RSTRIP.at[EDGE : EDGE + rows], strip_send.at[0], strip_recv.at[0], beside),
        remote(PS.at[rows - 8 : rows], RSTRIP.at[0:8], strip_send.at[1], strip_recv.at[1], diag_down),
        remote(PS.at[0:8], RSTRIP.at[nrow - 8 : nrow], strip_send.at[2], strip_recv.at[2], diag_up),
    ]

    def depth_of(mask, bed):
        return mask.astype(F32) * (1.0 + 0.5 * jnp.tanh(-bed))

    in_copies[5].wait()
    in_copies[6].wait()

    def depth_inner(i, carry):
        r = pl.multiple_of(i * R, R)
        D[pl.ds(r, R), 0:cols] = depth_of(MASK[pl.ds(r, R), 0:cols], BED[pl.ds(r, R), 0:cols])
        return carry

    lax.fori_loop(1, nblk - 1, depth_inner, 0)
    for copy in halo_copies:
        copy.wait_recv()
    for copy in strip_copies:
        copy.wait_recv()

    row_ids = lax.broadcasted_iota(jnp.int32, (R, LANE), 0)

    def unpack(i, carry):
        r = pl.multiple_of(i * R, R)
        strip = RSTRIP[pl.ds(r, R), :]
        inner = (lanes < HALO) & (tx == 0) | (lanes >= LANE - HALO) & (tx == 1)
        for k in range(8):
            shift = (LANE - HALO * k) * (1 - tx) + (LANE - HALO - HALO * k) * tx
            cells = jnp.where(inner, pltpu.roll(strip, shift % LANE, 1), 0.0)
            fields[k][pl.ds(r, R), cols:width] = cells.astype(fields[k].dtype)
        depth = depth_of(MASK[pl.ds(r, R), cols:width], BED[pl.ds(r, R), cols:width])
        at = row_ids + r
        real = ((at >= EDGE) | (ty > 0)) & ((at < EDGE + rows) | (ty < nty - 1))
        D[pl.ds(r, R), cols:width] = jnp.where(real, depth, 0.0)
        return carry

    lax.fori_loop(0, nblk, unpack, 0)
    wide_rows = lax.broadcasted_iota(jnp.int32, (R, cols), 0)
    for r in (0, nrow - R):
        depth = depth_of(MASK[r : r + R, 0:cols], BED[r : r + R, 0:cols])
        at = wide_rows + r
        real = ((at >= EDGE) | (ty > 0)) & ((at < EDGE + rows) | (ty < nty - 1))
        D[r : r + R, 0:cols] = jnp.where(real, depth, 0.0)

    for i in (0, 1, 2, 3, 4, 7):
        in_copies[i].wait()

    tide = par[0, 0] - 1.0
    fric = 0.2 * par[0, 1]
    coef = par[0, 2]
    flow_in = 0.3 * par[0, 3]
    keep = 1.0 - fric
    total = wts[0]
    for i in range(1, 16):
        total = total + wts[i]
    one = jnp.ones((1, width), F32)
    scale = one * (-4.0 * coef * wts[c].astype(F32)) / (one * total.astype(F32))

    def south(y):
        return pltpu.roll(y, R + 7, 0)[:R]

    def north(before, y):
        return pltpu.roll(jnp.concatenate([before, y], axis=0), 1, 0)[8:]

    def east(y):
        return pltpu.roll(y, width - 1, 1)

    def west(y):
        return pltpu.roll(y, 1, 1)

    def advance(step, i, carry):
        r = pl.multiple_of(i * R, R)
        here = pl.ds(r, R)
        level = E[pl.ds(r, R + 8), :]
        if step == 0:
            level = 0.3 * level
            deep = D[pl.ds(r, R + 8), :]
            depth = deep[:R]
            face_c = jnp.sqrt(depth * east(depth))
            face_r = jnp.sqrt(depth * south(deep))
            wet_c = face_c / (face_c + 0.1)
            wet_r = face_r / (face_r + 0.1)
            face_c = 0.3 * face_c
            face_r = 0.3 * face_r
            kind = CLS[here, :]
            relax = jnp.where(kind == 1, 0.5 * depth, 0.0)
            add = 0.3 * (relax * tide + flow_in * jnp.where(kind == 2, depth, 0.0))
            stay = 1.0 - relax
            WC[here, :] = wet_c
            WR[here, :] = wet_r
            FC[here, :] = face_c
            FR[here, :] = face_r
            A[here, :] = add
            B[here, :] = stay
        else:
            wet_c = WC[here, :]
            wet_r = WR[here, :]
            face_c = FC[here, :]
            face_r = FR[here, :]
            add = A[here, :]
            stay = B[here, :]
        mid = level[:R]
        vel_c = (keep * U[here, :] - (east(mid) - mid) + SX[here, :]) * wet_c
        vel_r = (keep * V[here, :] - (south(level) - mid) + SY[here, :]) * wet_r
        U[here, :] = vel_c
        V[here, :] = vel_r
        flux_c = face_c * vel_c
        flux_r = face_r * vel_r
        level = mid * stay + add - (flux_c - west(flux_c)) - (flux_r - north(carry[0], flux_r))
        if step == 2:
            level = level * (1.0 / 0.3)
        E[here, :] = level
        load_c = wet_c * vel_c * jnp.abs(vel_c)
        load_r = wet_r * vel_r * jnp.abs(vel_r)
        if step > 0:
            load_c = load_c + QC[here, :]
            load_r = load_r + QR[here, :]
        if step < 2:
            QC[here, :] = load_c
            QR[here, :] = load_r
            return (flux_r[R - 8 :],)
        T[here, :] = scale * (load_c - west(load_c) + load_r - north(carry[1], load_r))
        return (flux_r[R - 8 :], load_r[R - 8 :])

    done = [0, 0, 0]

    def run(step, stop):
        stop = min(stop, nblk)
        start = done[step]
        if stop <= start:
            return
        done[step] = stop
        if start == 0:
            carry = (jnp.zeros((8, width), F32),) * (2 if step == 2 else 1)
        else:
            carry = (CF[step],) + ((CQ[...],) if step == 2 else ())
        carry = lax.fori_loop(start, stop, functools.partial(advance, step), carry)
        if stop < nblk:
            CF[step] = carry[0]
            if step == 2:
                CQ[...] = carry[1]

    def pack_column():
        rolled = jnp.zeros((8, LANE), F32)
        lane8 = lax.broadcasted_iota(jnp.int32, (8, LANE), 1)
        sub8 = lax.broadcasted_iota(jnp.int32, (8, LANE), 0)

        def take(k, acc):
            cells = T[pl.ds(pl.multiple_of(EDGE + 8 * k, 8), 8), cols:width]
            cells = pltpu.roll(cells, (k + tx) % LANE, 1)
            return jnp.where(lane8 == k, cells, acc)

        rolled = lax.fori_loop(0, rows // 8, take, rolled)
        last = T[nrow - 8 : nrow, 0:LANE]
        T[nrow - 8 : nrow, 0:LANE] = jnp.where(sub8 == 0, last, rolled)
        last = T[nrow - 8 : nrow, LANE : 2 * LANE]
        T[nrow - 8 : nrow, LANE : 2 * LANE] = jnp.where(sub8 == 0, last, pltpu.roll(rolled, 1, 0))

    flying = {}
    sends = []

    def tile(k):
        r0 = sum(chunks[:k]) * R
        return r0, chunks[k] * R // 2

    def each(count, body):
        def loop(i, carry):
            body(pl.multiple_of(i * 8, 8))
            return carry

        lax.fori_loop(0, count // 8, loop, 0)

    def send(k, n, src, dst, peer):
        copy = remote(src, dst, ring_send.at[k, n], ring_recv.at[k, n], peer)
        flying[k, n] = copy
        sends.append(copy)

    def block(j):
        return pl.ds(pl.multiple_of(j * LANE, LANE), LANE)

    def piece(p):
        return pl.ds(pl.multiple_of(p * 2 * LANE, 2 * LANE), 2 * LANE)

    def stage0(k):
        r0, h = tile(k)
        h0 = r0 // 2
        theirs = pl.multiple_of(r0 + (1 - core) * h, 8)
        send(k, 0, T.at[pl.ds(theirs, h), 0:cols], CR.at[h0 : h0 + h], sibling)

    def stage1(k):
        r0, h = tile(k)
        h0 = r0 // 2
        mine = pl.multiple_of(r0 + core * h, 8)
        flying[k, 0].wait_recv()

        def body(i):
            at = pl.ds(h0 + i, 8)
            PP[at, :] = T[pl.ds(mine + i, 8), 0:cols] + CR[at, :]

        each(h, body)
        at = pl.ds(h0, h)
        send(k, 1, PP.at[at, block(2 * xf)], RAL.at[at], right)
        send(k, 2, PP.at[at, block(2 * xf + 1)], RAR.at[at], left)
        send(k, 3, PP.at[at, block(2 * xr + 1)], RBL.at[at], right)
        send(k, 4, PP.at[at, block(2 * xl)], RBR.at[at], left)

    def stage2(k):
        r0, h = tile(k)
        h0 = r0 // 2
        at = pl.ds(h0, h)
        flying[k, 1].wait_recv()

        def body1(i):
            at = pl.ds(h0 + i, 8)
            C1[at, :] = PP[at, block(2 * xr)] + RAL[at, :]

        each(h, body1)
        send(k, 5, C1.at[at], RCL.at[at], right)
        flying[k, 2].wait_recv()

        def body2(i):
            at = pl.ds(h0 + i, 8)
            C2[at, :] = PP[at, block(2 * xl + 1)] + RAR[at, :]

        each(h, body2)
        send(k, 6, C2.at[at], RCR.at[at], left)

    def stage3(k):
        r0, h = tile(k)
        h0 = r0 // 2
        at = pl.ds(h0, h)
        for n in (3, 4, 5, 6):
            flying[k, n].wait_recv()

        def body(i):
            at = pl.ds(h0 + i, 8)
            S[at, 0:LANE] = PP[at, block(2 * x)] + (RCL[at, :] + RBR[at, :])
            S[at, LANE : 2 * LANE] = PP[at, block(2 * x + 1)] + (RCR[at, :] + RBL[at, :])

        each(h, body)
        send(k, 7, S.at[at], RZ.at[at], zpeer)

    def stage4(k):
        r0, h = tile(k)
        h0 = r0 // 2
        mine = pl.multiple_of(r0 + core * h, 8)
        flying[k, 7].wait_recv()

        def body(i):
            at = pl.ds(h0 + i, 8)
            M[pl.ds(mine + i, 8), piece(x)] = S[at, :] + RZ[at, :]

        each(h, body)
        own = M.at[pl.ds(mine, h), piece(x)]
        send(k, 8, own, own, right)
        send(k, 9, own, own, left)
        send(k, 12, own, own, sibling)

    def stage5(k):
        r0, h = tile(k)
        mine = pl.multiple_of(r0 + core * h, 8)
        flying[k, 8].wait_recv()
        half = M.at[pl.ds(mine, h), block(2 * xl)]
        send(k, 10, half, half, right)
        flying[k, 9].wait_recv()
        half = M.at[pl.ds(mine, h), block(2 * xr + 1)]
        send(k, 11, half, half, left)
        for n, p in ((13, xl), (14, xr)):
            got = M.at[pl.ds(mine, h), piece(p)]
            send(k, n, got, got, sibling)

    def stage6(k):
        r0, h = tile(k)
        mine = pl.multiple_of(r0 + core * h, 8)
        flying[k, 10].wait_recv()
        flying[k, 11].wait_recv()
        got = M.at[pl.ds(mine, h), piece(xf)]
        send(k, 15, got, got, sibling)

    def stage7(k):
        for n in (12, 13, 14, 15):
            flying[k, n].wait_recv()

    stages = (stage0, stage1, stage2, stage3, stage4, stage5, stage6, stage7)
    at_stage = [0] * len(chunks)

    def progress(k):
        if at_stage[k] < len(stages):
            stages[at_stage[k]](k)
            at_stage[k] += 1

    for k in range(len(chunks)):
        stop = sum(chunks[: k + 1])
        run(0, stop + 2)
        run(1, stop + 1)
        run(2, stop)
        if k == len(chunks) - 1:
            pack_column()
        for j in range(k + 1):
            progress(j)
    state_copies = [
        pltpu.make_async_copy(field.at[EDGE : EDGE + rows, 0:cols], hy_h.at[0, i], out_sem.at[i])
        for i, field in enumerate((E, U, V))
    ]
    for copy in state_copies:
        copy.start()
    while min(at_stage) < len(stages):
        for k in range(len(chunks)):
            progress(k)

    change_copy = pltpu.make_async_copy(M.at[EDGE : EDGE + rows, 0:cols], bc_h, out_sem.at[3])
    change_copy.start()

    sub8 = lax.broadcasted_iota(jnp.int32, (8, LANE), 0)
    column = jnp.where(sub8 == 0, pltpu.roll(M[nrow - 8 : nrow, LANE : 2 * LANE], 7, 0), M[nrow - 8 : nrow, 0:LANE])

    def spread(k, carry):
        at = pl.ds(pl.multiple_of(EDGE + 8 * k, 8), 8)
        M[at, cols:width] = pltpu.roll(column, (2 * LANE - k - tx) % LANE, 1)
        return carry

    lax.fori_loop(0, rows // 8, spread, 0)

    place = lax.broadcasted_iota(jnp.int32, (R, width), 1)
    rows24 = lax.broadcasted_iota(jnp.int32, (R + 8, width), 0)
    inside_c = (place < cols) & (tx * cols + place <= ntx * cols - 2) | (place == width - 1) & (tx > 0)

    def bed_update(i, carry):
        r = pl.multiple_of(EDGE + i * R, 8)
        z = BED[pl.ds(r - 8, R + 16), :] + M[pl.ds(r - 8, R + 16), :]
        mid = z[8 : 8 + R]
        slope_c = jnp.where(inside_c, east(mid) - mid, 0.0)
        spill_c = 0.25 * (slope_c - jnp.clip(slope_c, -1.0, 1.0))
        top = z[: R + 8]
        at = rows24 + (ty * rows + i * R - 8)
        below_z = pltpu.roll(z, R + 15, 0)[: R + 8]
        slope_r = jnp.where((at >= 0) & (at <= nty * rows - 2), below_z - top, 0.0)
        spill_r = 0.25 * (slope_r - jnp.clip(slope_r, -1.0, 1.0))
        flow_r = (spill_r - pltpu.roll(spill_r, 1, 0))[8:]
        bed_new = mid + (spill_c - west(spill_c)) + flow_r
        BN[pl.ds(i * R, R), :] = bed_new[:, 0:cols]
        return carry

    lax.fori_loop(0, rows // R, bed_update, 0)
    bed_copy = pltpu.make_async_copy(BN, bn_h, out_sem.at[4])
    bed_copy.start()
    for copy in halo_copies + strip_copies + sends:
        copy.wait_send()
    for copy in state_copies:
        copy.wait()
    change_copy.wait()
    bed_copy.wait()


def shards(bed, land_mask, cell_class, weights, cond_params, wave_stress, hydro_state):
    rows, cols = bed.shape
    chunks = CHUNKS
    nrow, width = rows + 2 * EDGE, cols + LANE
    assert sum(chunks) * R == nrow
    half = nrow // 2
    vm = pltpu.VMEM
    full = vm((nrow, width), F32)
    tall = vm((nrow + 8, width), F32)
    ints = vm((nrow, width), jnp.int32)
    thin = vm((half, LANE), F32)
    dma = pltpu.SemaphoreType.DMA
    hbm = pl.BlockSpec(memory_space=pl.ANY)
    smem = pl.BlockSpec(memory_space=pltpu.SMEM)
    return pl.pallas_call(
        functools.partial(kernel, rows, cols, chunks),
        out_shape=(
            jax.ShapeDtypeStruct((rows, cols), F32),
            jax.ShapeDtypeStruct((rows, cols), F32),
            jax.ShapeDtypeStruct(hydro_state.shape, F32),
        ),
        in_specs=[hbm, hbm, hbm, smem, smem, hbm, hbm],
        out_specs=(hbm, hbm, hbm),
        scratch_shapes=[
            tall, full, full, full, full, full, ints, ints,
            tall, full, full, full, full, full, full, full, full,
            full, full, vm((rows, cols), F32),
            vm((3, 8, width), F32), vm((8, width), F32),
            vm((6, rows, LANE), F32), vm((2, rows, LANE), jnp.int32),
            vm((rows, LANE), F32), vm((nrow, LANE), F32),
            vm((half, cols), F32), vm((half, cols), F32),
            thin, thin, thin, thin, thin, thin, thin, thin,
            vm((half, 2 * LANE), F32), vm((half, 2 * LANE), F32),
            dma((8,)), dma((8,)), dma((2, 8)), dma((2, 8)), dma((3,)), dma((3,)),
            dma((len(chunks), 16)), dma((len(chunks), 16)), dma((5,)),
        ],
        compiler_params=pltpu.CompilerParams(
            collective_id=0, has_side_effects=True, vmem_limit_bytes=60 * 1024 * 1024
        ),
    )(bed, land_mask, cell_class, weights, cond_params, wave_stress, hydro_state)


def solution(mesh):
    in_specs = (
        P("ty", "tx"),
        P("ty", "tx"),
        P("ty", "tx"),
        P(),
        P("cond", None),
        P("cond", None, "ty", "tx"),
        P("cond", None, "ty", "tx"),
    )
    out_specs = (P("ty", "tx"), P("ty", "tx"), P("cond", None, "ty", "tx"))
    return jax.shard_map(shards, mesh=mesh, in_specs=in_specs, out_specs=out_specs, check_vma=False)
```

```python
import functools

import jax
import jax.numpy as jnp
from jax import lax
from jax.experimental import pallas as pl
from jax.experimental.pallas import tpu as pltpu
from jax.sharding import PartitionSpec as P

MESH = pl.DeviceIdType.MESH
F32 = jnp.float32
LANE = 128
EDGE = 8
HALO = 4
GROUPS = 4
R = 16
NX = 4
FAR_FIRST = ((1, 2), (1, 1), (1, 3), (0, 2), (1, 0), (0, 1), (0, 3))
PIN = True
MERGE_VMEM = 56 << 20
FINISH_VMEM = 16 << 20
CHUNKS = (10, 7)
SCHEDULE = ((10, (0,)), (13, (0,)), (17, (1, 0, 1, 0, 1)))


def east(y):
    return pltpu.roll(y, y.shape[1] - 1, 1)


def west(y):
    return pltpu.roll(y, 1, 1)


def kernel(
    rows,
    cols,
    chunks,
    schedule,
    bed_h,
    mask_h,
    cls_h,
    wts,
    par,
    stress_h,
    hydro_h,
    E,
    U,
    V,
    BED,
    M,
    SX,
    SY,
    MASK,
    CLS,
    D,
    WC,
    WR,
    FC,
    FR,
    A,
    B,
    QC,
    QR,
    T,
    CF,
    CQ,
    EDF,
    EDI,
    PS,
    RSTRIP,
    CR,
    PP,
    RX,
    in_sem,
    edge_sem,
    halo_send,
    halo_recv,
    strip_send,
    strip_recv,
    ring_send,
    ring_recv,
):
    nrow = rows + 2 * EDGE
    width = cols + LANE
    nblk = nrow // R
    c = lax.axis_index("cond")
    ty = lax.axis_index("ty")
    tx = lax.axis_index("tx")
    nty = lax.axis_size("ty")
    ntx = lax.axis_size("tx")
    core = c % 2
    x = (c // 2) % NX
    zh = c // (2 * NX)
    up = (ty + nty - 1) % nty
    down = (ty + 1) % nty
    side = 1 - tx

    def cond_of(z, xx, k):
        return (z * NX + xx) * 2 + k

    sibling = (cond_of(zh, x, 1 - core), ty, tx)
    chips = [((zh + dz) % 2, (x + dx) % NX) for dz, dx in FAR_FIRST]
    partners = [(cond_of(z, xx, core), ty, tx) for z, xx in chips]
    parts = [z * NX + xx for z, xx in chips]
    own_part = zh * NX + x
    above = (c, up, tx)
    below = (c, down, tx)
    beside = (c, ty, side)
    diag_up = (c, up, side)
    diag_down = (c, down, side)

    fields = (E, U, V, SX, SY, BED, MASK, CLS)
    sources = (
        hydro_h.at[0, 0],
        hydro_h.at[0, 1],
        hydro_h.at[0, 2],
        stress_h.at[0, 0],
        stress_h.at[0, 1],
        bed_h,
        mask_h,
        cls_h,
    )
    edge_at = pl.multiple_of((1 - tx) * (cols - LANE), LANE)
    edges = [EDF.at[i] for i in range(6)] + [EDI.at[i] for i in range(2)]

    edge_copies = [
        pltpu.make_async_copy(src.at[:, pl.ds(edge_at, LANE)], dst, edge_sem.at[i])
        for i, (src, dst) in enumerate(zip(sources, edges))
    ]
    for copy in edge_copies:
        copy.start()
    in_copies = [
        pltpu.make_async_copy(src, dst.at[EDGE : EDGE + rows, 0:cols], in_sem.at[i])
        for i, (src, dst) in enumerate(zip(sources, fields))
    ]
    for i in (5, 6, 0, 1, 2, 3, 4, 7):
        in_copies[i].start()

    barrier = pltpu.get_barrier_semaphore()
    peers = (sibling, *partners, above, below, beside, diag_up, diag_down)
    for peer in peers:
        pl.semaphore_signal(barrier, inc=1, device_id=peer, device_id_type=MESH)
    pad = EDGE - HALO
    for field in fields:
        field[0:pad, 0:cols] = jnp.zeros((pad, cols), field.dtype)
        field[nrow - pad : nrow, 0:cols] = jnp.zeros((pad, cols), field.dtype)
    E[nrow : nrow + 8, :] = jnp.zeros((8, width), F32)
    D[nrow : nrow + 8, :] = jnp.zeros((8, width), F32)
    pl.semaphore_wait(barrier, len(peers))

    def remote(src, dst, send, recv, peer):
        copy = pltpu.make_async_remote_copy(
            src_ref=src, dst_ref=dst, send_sem=send, recv_sem=recv, device_id=peer, device_id_type=MESH
        )
        copy.start()
        return copy

    halo_copies = []
    for i, (src, dst) in enumerate(zip(sources, fields)):
        halo_copies.append(
            remote(
                src.at[rows - HALO : rows, :],
                dst.at[EDGE - HALO : EDGE, 0:cols],
                halo_send.at[0, i],
                halo_recv.at[0, i],
                below,
            )
        )
        halo_copies.append(
            remote(
                src.at[0:HALO, :],
                dst.at[EDGE + rows : EDGE + rows + HALO, 0:cols],
                halo_send.at[1, i],
                halo_recv.at[1, i],
                above,
            )
        )

    lanes = lax.broadcasted_iota(jnp.int32, (R, LANE), 1)
    for copy in edge_copies:
        copy.wait()

    group = rows // GROUPS

    def pack(i, carry):
        strip = jnp.zeros((R, LANE), F32)
        for g in range(GROUPS):
            r = pl.multiple_of(g * group + i * R, R)
            for k in range(8):
                first = (g * 8 + k) * HALO
                cells = edges[k][pl.ds(r, R), :].astype(F32)
                cells = pltpu.roll(cells, (first + HALO * (1 - tx)) % LANE, 1)
                strip = jnp.where((lanes >= first) & (lanes < first + HALO), cells, strip)
        PS[pl.ds(pl.multiple_of(i * R, R), R), :] = strip
        return carry

    lax.fori_loop(0, group // R, pack, 0)
    strip_copies = [
        remote(PS, RSTRIP.at[8 : 8 + group], strip_send.at[0], strip_recv.at[0], beside),
        remote(PS.at[group - 8 : group], RSTRIP.at[0:8], strip_send.at[1], strip_recv.at[1], diag_down),
        remote(PS.at[0:8], RSTRIP.at[group + 8 : group + 16], strip_send.at[2], strip_recv.at[2], diag_up),
    ]

    def depth_of(mask, bed):
        return mask.astype(F32) * (1.0 + 0.5 * jnp.tanh(-bed))

    in_copies[5].wait()
    in_copies[6].wait()

    def depth_inner(i, carry):
        r = pl.multiple_of(i * R, R)
        D[pl.ds(r, R), 0:cols] = depth_of(MASK[pl.ds(r, R), 0:cols], BED[pl.ds(r, R), 0:cols])
        return carry

    lax.fori_loop(1, nblk - 1, depth_inner, 0)
    for copy in halo_copies:
        copy.wait_recv()
    for copy in strip_copies:
        copy.wait_recv()

    def unpack(n, src, dst, g, real):
        strip = RSTRIP[pl.ds(src, n), :]
        lane = lanes[:n]
        inner = (lane < HALO) & (tx == 0) | (lane >= LANE - HALO) & (tx == 1)
        at = pl.ds(dst, n)
        parts = []
        for k in range(8):
            shift = 2 * LANE - (g * 8 + k) * HALO - HALO * tx
            cells = jnp.where(inner, pltpu.roll(strip, shift % LANE, 1), 0.0)
            parts.append(cells.astype(fields[k].dtype))
            fields[k][at, cols:width] = parts[k]
        depth = depth_of(parts[6], parts[5])
        D[at, cols:width] = depth if real is None else jnp.where(real, depth, 0.0)

    def unpack_rows(i, carry):
        for g in range(GROUPS):
            r = pl.multiple_of(i * R, R)
            unpack(R, 8 + r, pl.multiple_of(EDGE + g * group + r, 8), g, None)
        return carry

    lax.fori_loop(0, group // R, unpack_rows, 0)
    unpack(8, 0, 0, GROUPS - 1, ty > 0)
    unpack(8, group + 8, nrow - 8, 0, ty < nty - 1)
    wide_rows = lax.broadcasted_iota(jnp.int32, (R, cols), 0)
    for r in (0, nrow - R):
        depth = depth_of(MASK[r : r + R, 0:cols], BED[r : r + R, 0:cols])
        at = wide_rows + r
        real = ((at >= EDGE) | (ty > 0)) & ((at < EDGE + rows) | (ty < nty - 1))
        D[r : r + R, 0:cols] = jnp.where(real, depth, 0.0)

    for i in (0, 1, 2, 3, 4, 7):
        in_copies[i].wait()

    tide = par[0, 0] - 1.0
    fric = 0.2 * par[0, 1]
    coef = par[0, 2]
    flow_in = 0.3 * par[0, 3]
    keep = 1.0 - fric
    total = wts[0]
    for i in range(1, 16):
        total = total + wts[i]
    one = jnp.ones((1, width), F32)
    scale = one * (-4.0 * coef * wts[c].astype(F32)) / (one * total.astype(F32))

    def south(y):
        return pltpu.roll(y, R + 7, 0)[:R]

    def north(before, y):
        return pltpu.roll(jnp.concatenate([before, y], axis=0), 1, 0)[8:]

    def advance(step, i, carry):
        r = pl.multiple_of(i * R, R)
        here = pl.ds(r, R)
        level = E[pl.ds(r, R + 8), :]
        if step == 0:
            level = 0.3 * level
            deep = D[pl.ds(r, R + 8), :]
            depth = deep[:R]
            face_c = jnp.sqrt(depth * east(depth))
            face_r = jnp.sqrt(depth * south(deep))
            wet_c = face_c / (face_c + 0.1)
            wet_r = face_r / (face_r + 0.1)
            face_c = 0.3 * face_c
            face_r = 0.3 * face_r
            kind = CLS[here, :]
            relax = jnp.where(kind == 1, 0.5 * depth, 0.0)
            add = 0.3 * (relax * tide + flow_in * jnp.where(kind == 2, depth, 0.0))
            stay = 1.0 - relax
            WC[here, :] = wet_c
            WR[here, :] = wet_r
            FC[here, :] = face_c
            FR[here, :] = face_r
            A[here, :] = add
            B[here, :] = stay
        else:
            wet_c = WC[here, :]
            wet_r = WR[here, :]
            face_c = FC[here, :]
            face_r = FR[here, :]
            add = A[here, :]
            stay = B[here, :]
        mid = level[:R]
        vel_c = (keep * U[here, :] - (east(mid) - mid) + SX[here, :]) * wet_c
        vel_r = (keep * V[here, :] - (south(level) - mid) + SY[here, :]) * wet_r
        U[here, :] = vel_c
        V[here, :] = vel_r
        flux_c = face_c * vel_c
        flux_r = face_r * vel_r
        level = mid * stay + add - (flux_c - west(flux_c)) - (flux_r - north(carry[0], flux_r))
        if step == 2:
            level = level * (1.0 / 0.3)
        E[here, :] = level
        load_c = wet_c * vel_c * jnp.abs(vel_c)
        load_r = wet_r * vel_r * jnp.abs(vel_r)
        if step > 0:
            load_c = load_c + QC[here, :]
            load_r = load_r + QR[here, :]
        if step < 2:
            QC[here, :] = load_c
            QR[here, :] = load_r
            return (flux_r[R - 8 :],)
        T[here, :] = scale * (load_c - west(load_c) + load_r - north(carry[1], load_r))
        return (flux_r[R - 8 :], load_r[R - 8 :])

    done = [0, 0, 0]

    def run(step, stop):
        stop = min(stop, nblk)
        start = done[step]
        if stop <= start:
            return
        done[step] = stop
        if start == 0:
            carry = (jnp.zeros((8, width), F32),) * (2 if step == 2 else 1)
        else:
            carry = (CF[step],) + ((CQ[...],) if step == 2 else ())
        carry = lax.fori_loop(start, stop, functools.partial(advance, step), carry)
        if stop < nblk:
            CF[step] = carry[0]
            if step == 2:
                CQ[...] = carry[1]

    def pack_column():
        rolled = jnp.zeros((8, LANE), F32)
        lane8 = lax.broadcasted_iota(jnp.int32, (8, LANE), 1)
        sub8 = lax.broadcasted_iota(jnp.int32, (8, LANE), 0)

        def take(k, acc):
            cells = T[pl.ds(pl.multiple_of(EDGE + 8 * k, 8), 8), cols:width]
            cells = pltpu.roll(cells, (k + tx) % LANE, 1)
            return jnp.where(lane8 == k, cells, acc)

        rolled = lax.fori_loop(0, rows // 8, take, rolled, unroll=8)
        last = T[nrow - 8 : nrow, 0:LANE]
        T[nrow - 8 : nrow, 0:LANE] = jnp.where(sub8 == 0, last, rolled)
        last = T[nrow - 8 : nrow, LANE : 2 * LANE]
        T[nrow - 8 : nrow, LANE : 2 * LANE] = jnp.where(sub8 == 0, last, pltpu.roll(rolled, 1, 0))

    flying = {}
    sends = []

    def tile(k):
        r0 = sum(chunks[:k]) * R
        return r0, chunks[k] * R // 2

    def each(count, body):
        def loop(i, carry):
            body(pl.multiple_of(i * 8, 8))
            return carry

        lax.fori_loop(0, count // 8, loop, 0)

    def send(k, n, src, dst, peer):
        copy = remote(src, dst, ring_send.at[k, n], ring_recv.at[k, n], peer)
        flying[k, n] = copy
        sends.append(copy)

    def block(j):
        return pl.ds(pl.multiple_of(j * LANE, LANE), LANE)

    def stage0(k):
        r0, h = tile(k)
        h0 = r0 // 2
        theirs = pl.multiple_of(r0 + (1 - core) * h, 8)
        send(k, 0, T.at[pl.ds(theirs, h), 0:cols], CR.at[h0 : h0 + h], sibling)

    def stage1(k):
        r0, h = tile(k)
        h0 = r0 // 2
        mine = pl.multiple_of(r0 + core * h, 8)
        flying[k, 0].wait_recv()

        def body(i):
            at = pl.ds(h0 + i, 8)
            PP[at, :] = T[pl.ds(mine + i, 8), 0:cols] + CR[at, :]

        each(h, body)
        at = pl.ds(h0, h)
        for n, partner in enumerate(partners):
            send(k, 1 + n, PP.at[at, block(parts[n])], RX.at[n, at], partner)

    def stage2(k):
        r0, h = tile(k)
        h0 = r0 // 2
        mine = pl.multiple_of(r0 + core * h, 8)
        for n in range(len(partners)):
            flying[k, 1 + n].wait_recv()

        def body(i):
            at = pl.ds(h0 + i, 8)
            acc = PP[at, block(own_part)]
            for n in range(len(partners)):
                acc = acc + RX[n, at, :]
            M[pl.ds(mine + i, 8), block(own_part)] = acc

        each(h, body)
        own = M.at[pl.ds(mine, h), block(own_part)]
        for n, partner in enumerate(partners):
            send(k, 8 + n, own, own, partner)

    def stage3(k):
        r0, h = tile(k)
        mine = pl.multiple_of(r0 + core * h, 8)
        for n in range(len(partners)):
            flying[k, 8 + n].wait_recv()
        got = M.at[pl.ds(mine, h), 0:cols]
        send(k, 15, got, got, sibling)

    def stage4(k):
        flying[k, 15].wait_recv()

    stages = (stage0, stage1, stage2, stage3, stage4)
    at_stage = [0] * len(chunks)

    def progress(k):
        if at_stage[k] < len(stages):
            stages[at_stage[k]](k)
            at_stage[k] += 1

    for stop, ready in schedule:
        run(0, stop + 2)
        run(1, stop + 1)
        run(2, stop)
        if stop == nblk:
            pack_column()
        for k in ready:
            progress(k)
    while min(at_stage) < len(stages):
        for k in range(len(chunks)):
            progress(k)

    for copy in halo_copies + strip_copies + sends:
        copy.wait_send()


def finish(rows, cols, E, U, V, BED, M, bn_h, bc_h, hy_h, Z, BN, out_sem):
    nrow = rows + 2 * EDGE
    width = cols + LANE
    ty = lax.axis_index("ty")
    tx = lax.axis_index("tx")
    nty = lax.axis_size("ty")
    ntx = lax.axis_size("tx")
    copies = [
        pltpu.make_async_copy(field.at[EDGE : EDGE + rows, 0:cols], hy_h.at[0, i], out_sem.at[i])
        for i, field in enumerate((E, U, V))
    ]
    copies.append(pltpu.make_async_copy(M.at[EDGE : EDGE + rows, 0:cols], bc_h, out_sem.at[3]))
    for copy in copies:
        copy.start()

    sub8 = lax.broadcasted_iota(jnp.int32, (8, LANE), 0)
    column = jnp.where(sub8 == 0, pltpu.roll(M[nrow - 8 : nrow, LANE : 2 * LANE], 7, 0), M[nrow - 8 : nrow, 0:LANE])

    def spread(k, carry):
        at = pl.ds(pl.multiple_of(EDGE + 8 * k, 8), 8)
        Z[at, :] = pltpu.roll(column, (2 * LANE - k - tx) % LANE, 1)
        return carry

    Z[0:EDGE, :] = jnp.zeros((EDGE, LANE), F32)
    Z[nrow - EDGE : nrow, :] = jnp.zeros((EDGE, LANE), F32)
    lax.fori_loop(0, rows // 8, spread, 0, unroll=8)

    place = lax.broadcasted_iota(jnp.int32, (R, width), 1)
    rows24 = lax.broadcasted_iota(jnp.int32, (R + 8, width), 0)
    inside_c = (place < cols) & (tx * cols + place <= ntx * cols - 2) | (place == width - 1) & (tx > 0)

    def bed_update(i, carry):
        r = pl.multiple_of(EDGE + i * R, 8)
        at = pl.ds(r - 8, R + 16)
        z = BED[at, :] + jnp.concatenate([M[at, :], Z[at, :]], axis=1)
        mid = z[8 : 8 + R]
        slope_c = jnp.where(inside_c, east(mid) - mid, 0.0)
        spill_c = 0.25 * (slope_c - jnp.clip(slope_c, -1.0, 1.0))
        top = z[: R + 8]
        at = rows24 + (ty * rows + i * R - 8)
        below_z = pltpu.roll(z, R + 15, 0)[: R + 8]
        slope_r = jnp.where((at >= 0) & (at <= nty * rows - 2), below_z - top, 0.0)
        spill_r = 0.25 * (slope_r - jnp.clip(slope_r, -1.0, 1.0))
        flow_r = (spill_r - pltpu.roll(spill_r, 1, 0))[8:]
        bed_new = mid + (spill_c - west(spill_c)) + flow_r
        BN[pl.ds(i * R, R), :] = bed_new[:, 0:cols]
        return carry

    lax.fori_loop(0, rows // R, bed_update, 0)
    copies.append(pltpu.make_async_copy(BN, bn_h, out_sem.at[4]))
    copies[-1].start()
    for copy in copies:
        copy.wait()


def pinned(ref):
    return ref if PIN else jax.ShapeDtypeStruct(ref.shape, ref.dtype)


def shards(bed, land_mask, cell_class, weights, cond_params, wave_stress, hydro_state):
    rows, cols = bed.shape
    chunks = CHUNKS
    nrow, width = rows + 2 * EDGE, cols + LANE
    assert sum(chunks) * R == nrow
    half = nrow // 2
    vm = pltpu.VMEM
    full = vm((nrow, width), F32)
    tall = vm((nrow + 8, width), F32)
    ints = vm((nrow, width), jnp.int32)
    dma = pltpu.SemaphoreType.DMA
    hbm = pl.BlockSpec(memory_space=pltpu.HBM)
    smem = pl.BlockSpec(memory_space=pltpu.SMEM)
    vmem = pl.BlockSpec(memory_space=pltpu.VMEM)
    merge = pl.pallas_call(
        functools.partial(kernel, rows, cols, chunks, SCHEDULE),
        out_shape=tuple(pinned(ref) for ref in (tall, full, full, full, vm((nrow, cols), F32))),
        in_specs=[hbm, hbm, hbm, smem, smem, hbm, hbm],
        out_specs=(vmem,) * 5,
        scratch_shapes=[
            full, full, ints, ints,
            tall, full, full, full, full, full, full, full, full, full,
            vm((3, 8, width), F32), vm((8, width), F32),
            vm((6, rows, LANE), F32), vm((2, rows, LANE), jnp.int32),
            vm((rows // GROUPS, LANE), F32), vm((rows // GROUPS + 16, LANE), F32),
            vm((half, cols), F32), vm((half, cols), F32), vm((7, half, LANE), F32),
            dma((8,)), dma((8,)), dma((2, 8)), dma((2, 8)), dma((3,)), dma((3,)),
            dma((len(chunks), 16)), dma((len(chunks), 16)),
        ],
        compiler_params=pltpu.CompilerParams(
            collective_id=0, has_side_effects=True, vmem_limit_bytes=MERGE_VMEM
        ),
        name="merge",
    )
    fields = merge(bed, land_mask, cell_class, weights, cond_params, wave_stress, hydro_state)
    if PIN:
        fields = [pltpu.with_memory_space_constraint(field, pltpu.VMEM) for field in fields]
    return pl.pallas_call(
        functools.partial(finish, rows, cols),
        out_shape=(
            jax.ShapeDtypeStruct((rows, cols), F32),
            jax.ShapeDtypeStruct((rows, cols), F32),
            jax.ShapeDtypeStruct(hydro_state.shape, F32),
        ),
        in_specs=[vmem] * 5,
        out_specs=(hbm, hbm, hbm),
        scratch_shapes=[vm((nrow, LANE), F32), vm((rows, cols), F32), dma((5,))],
        compiler_params=pltpu.CompilerParams(vmem_limit_bytes=FINISH_VMEM),
        name="finish",
    )(*fields)


def solution(mesh):
    in_specs = (
        P("ty", "tx"),
        P("ty", "tx"),
        P("ty", "tx"),
        P(),
        P("cond", None),
        P("cond", None, "ty", "tx"),
        P("cond", None, "ty", "tx"),
    )
    out_specs = (P("ty", "tx"), P("ty", "tx"), P("cond", None, "ty", "tx"))
    return jax.shard_map(shards, mesh=mesh, in_specs=in_specs, out_specs=out_specs, check_vma=False)
```

```python
import functools

import jax
import jax.numpy as jnp
from jax import lax
from jax.experimental import pallas as pl
from jax.experimental.pallas import tpu as pltpu
from jax.sharding import PartitionSpec as P

MESH = pl.DeviceIdType.MESH
F32 = jnp.float32
LANE = 128
EDGE = 8
HALO = 4
GROUPS = 4
R = 16
NX = 4
FAR_FIRST = ((1, 2), (1, 1), (1, 3), (0, 2), (1, 0), (0, 1), (0, 3))
SKEW = 2
PIN = True
MERGE_VMEM = 56 << 20
FINISH_VMEM = 16 << 20
CHUNKS = (10, 7)
SCHEDULE = ((10, (0,)), (13, (0,)), (17, (1, 1, 0, 1, 0, 1, 0, 1)))


def east(y):
    return pltpu.roll(y, y.shape[1] - 1, 1)


def west(y):
    return pltpu.roll(y, 1, 1)


def kernel(
    rows,
    cols,
    chunks,
    schedule,
    bed_h,
    mask_h,
    cls_h,
    wts_h,
    par_h,
    stress_h,
    hydro_h,
    E3,
    U3,
    V3,
    BED,
    M,
    E,
    E1,
    E2,
    U,
    U1,
    U2,
    V,
    V1,
    V2,
    SX,
    SY,
    MASK,
    CLS,
    D,
    WC,
    WR,
    FC,
    FR,
    A,
    B,
    QC,
    QC1,
    QR,
    QR1,
    T,
    CF,
    CQ,
    EDF,
    EDI,
    PS,
    RSTRIP,
    CR,
    PP,
    RX,
    wts,
    par,
    small_sem,
    in_sem,
    edge_sem,
    halo_send,
    halo_recv,
    strip_send,
    strip_recv,
    ring_send,
    ring_recv,
):
    nrow = rows + 2 * EDGE
    width = cols + LANE
    nblk = nrow // R
    c = lax.axis_index("cond")
    ty = lax.axis_index("ty")
    tx = lax.axis_index("tx")
    nty = lax.axis_size("ty")
    ntx = lax.axis_size("tx")
    core = c % 2
    x = (c // 2) % NX
    zh = c // (2 * NX)
    up = (ty + nty - 1) % nty
    down = (ty + 1) % nty
    side = 1 - tx

    def cond_of(z, xx, k):
        return (z * NX + xx) * 2 + k

    sibling = (cond_of(zh, x, 1 - core), ty, tx)
    chips = [((zh + dz) % 2, (x + dx) % NX) for dz, dx in FAR_FIRST]
    partners = [(cond_of(z, xx, core), ty, tx) for z, xx in chips]
    parts = [z * NX + xx for z, xx in chips]
    own_part = zh * NX + x
    above = (c, up, tx)
    below = (c, down, tx)
    beside = (c, ty, side)
    diag_up = (c, up, side)
    diag_down = (c, down, side)

    fields = (E, U, V, SX, SY, BED, MASK, CLS)
    sources = (
        hydro_h.at[0, 0],
        hydro_h.at[0, 1],
        hydro_h.at[0, 2],
        stress_h.at[0, 0],
        stress_h.at[0, 1],
        bed_h,
        mask_h,
        cls_h,
    )
    edge_at = pl.multiple_of((1 - tx) * (cols - LANE), LANE)
    edges = [EDF.at[i] for i in range(6)] + [EDI.at[i] for i in range(2)]

    small_copies = [
        pltpu.make_async_copy(wts_h, wts, small_sem.at[0]),
        pltpu.make_async_copy(par_h, par, small_sem.at[1]),
    ]
    for copy in small_copies:
        copy.start()
    edge_copies = [
        pltpu.make_async_copy(src.at[:, pl.ds(edge_at, LANE)], dst, edge_sem.at[i])
        for i, (src, dst) in enumerate(zip(sources, edges))
    ]
    for copy in edge_copies:
        copy.start()
    in_copies = [
        pltpu.make_async_copy(src, dst.at[EDGE : EDGE + rows, 0:cols], in_sem.at[i])
        for i, (src, dst) in enumerate(zip(sources, fields))
    ]
    for i in (5, 6, 0, 1, 2, 3, 4, 7):
        in_copies[i].start()

    barrier = pltpu.get_barrier_semaphore()
    peers = (sibling, *partners, above, below, beside, diag_up, diag_down)
    for peer in peers:
        pl.semaphore_signal(barrier, inc=1, device_id=peer, device_id_type=MESH)
    pad = EDGE - HALO
    for field in fields:
        field[0:pad, 0:cols] = jnp.zeros((pad, cols), field.dtype)
        field[nrow - pad : nrow, 0:cols] = jnp.zeros((pad, cols), field.dtype)
    for level in (E, E1, E2):
        level[nrow : nrow + 8, :] = jnp.zeros((8, width), F32)
    D[nrow : nrow + 8, :] = jnp.zeros((8, width), F32)
    pl.semaphore_wait(barrier, len(peers))

    def remote(src, dst, send, recv, peer):
        copy = pltpu.make_async_remote_copy(
            src_ref=src, dst_ref=dst, send_sem=send, recv_sem=recv, device_id=peer, device_id_type=MESH
        )
        copy.start()
        return copy

    halo_copies = []
    for i, (src, dst) in enumerate(zip(sources, fields)):
        halo_copies.append(
            remote(
                src.at[rows - HALO : rows, :],
                dst.at[EDGE - HALO : EDGE, 0:cols],
                halo_send.at[0, i],
                halo_recv.at[0, i],
                below,
            )
        )
        halo_copies.append(
            remote(
                src.at[0:HALO, :],
                dst.at[EDGE + rows : EDGE + rows + HALO, 0:cols],
                halo_send.at[1, i],
                halo_recv.at[1, i],
                above,
            )
        )

    lanes = lax.broadcasted_iota(jnp.int32, (R, LANE), 1)
    for copy in edge_copies:
        copy.wait()

    group = rows // GROUPS

    def pack(i, carry):
        strip = jnp.zeros((R, LANE), F32)
        for g in range(GROUPS):
            r = pl.multiple_of(g * group + i * R, R)
            for k in range(8):
                first = (g * 8 + k) * HALO
                cells = edges[k][pl.ds(r, R), :].astype(F32)
                cells = pltpu.roll(cells, (first + HALO * (1 - tx)) % LANE, 1)
                strip = jnp.where((lanes >= first) & (lanes < first + HALO), cells, strip)
        PS[pl.ds(pl.multiple_of(i * R, R), R), :] = strip
        return carry

    lax.fori_loop(0, group // R, pack, 0)
    strip_copies = [
        remote(PS, RSTRIP.at[8 : 8 + group], strip_send.at[0], strip_recv.at[0], beside),
        remote(PS.at[group - 8 : group], RSTRIP.at[0:8], strip_send.at[1], strip_recv.at[1], diag_down),
        remote(PS.at[0:8], RSTRIP.at[group + 8 : group + 16], strip_send.at[2], strip_recv.at[2], diag_up),
    ]

    def depth_of(mask, bed):
        return mask.astype(F32) * (1.0 + 0.5 * jnp.tanh(-bed))

    in_copies[5].wait()
    in_copies[6].wait()

    def depth_inner(i, carry):
        at = pl.ds(pl.multiple_of(EDGE + i * R, 8), R)
        D[at, 0:cols] = depth_of(MASK[at, 0:cols], BED[at, 0:cols])
        return carry

    lax.fori_loop(0, rows // R, depth_inner, 0)

    for copy in small_copies:
        copy.wait()
    in_copies[7].wait()
    tide = par[0, 0] - 1.0
    fric = 0.2 * par[0, 1]
    coef = par[0, 2]
    flow_in = 0.3 * par[0, 3]
    keep = 1.0 - fric

    def faces(depth, beyond, face, wet, at, span):
        root = jnp.sqrt(depth * beyond)
        wet[at, span] = root / (root + 0.1)
        face[at, span] = 0.3 * root

    def level_terms(depth, at, span):
        kind = CLS[at, span]
        relax = jnp.where(kind == 1, 0.5 * depth, 0.0)
        A[at, span] = 0.3 * (relax * tide + flow_in * jnp.where(kind == 2, depth, 0.0))
        B[at, span] = 1.0 - relax

    def prepare(r, n, span):
        at = pl.ds(r, n)
        deep = D[pl.ds(r, n + 8), span]
        depth = deep[:n]
        faces(depth, east(depth), FC, WC, at, span)
        faces(depth, pltpu.roll(deep, n + 7, 0)[:n], FR, WR, at, span)
        level_terms(depth, at, span)

    def prepare_inner(i, carry):
        prepare(pl.multiple_of(i * R, R), R, slice(0, cols))
        return carry

    lax.fori_loop(1, nblk - 1, prepare_inner, 0)
    for copy in halo_copies:
        copy.wait_recv()
    for copy in strip_copies:
        copy.wait_recv()

    def unpack(n, src, dst, g, real):
        strip = RSTRIP[pl.ds(src, n), :]
        lane = lanes[:n]
        inner = (lane < HALO) & (tx == 0) | (lane >= LANE - HALO) & (tx == 1)
        at = pl.ds(dst, n)
        parts = []
        for k in range(8):
            shift = 2 * LANE - (g * 8 + k) * HALO - HALO * tx
            cells = jnp.where(inner, pltpu.roll(strip, shift % LANE, 1), 0.0)
            parts.append(cells.astype(fields[k].dtype))
            fields[k][at, cols:width] = parts[k]
        depth = depth_of(parts[6], parts[5])
        D[at, cols:width] = depth if real is None else jnp.where(real, depth, 0.0)

    def unpack_rows(i, carry):
        for g in range(GROUPS):
            r = pl.multiple_of(i * R, R)
            unpack(R, 8 + r, pl.multiple_of(EDGE + g * group + r, 8), g, None)
        return carry

    lax.fori_loop(0, group // R, unpack_rows, 0)
    unpack(8, 0, 0, GROUPS - 1, ty > 0)
    unpack(8, group + 8, nrow - 8, 0, ty < nty - 1)
    for r, real in ((0, ty > 0), (nrow - 8, ty < nty - 1)):
        depth = depth_of(MASK[r : r + 8, 0:cols], BED[r : r + 8, 0:cols])
        D[r : r + 8, 0:cols] = jnp.where(real, depth, 0.0)
    for r in (0, nrow - R):
        prepare(r, R, slice(0, width))

    tall_block = (nblk - 2) * R // 3

    def prepare_edge(i, carry):
        r = pl.multiple_of(R + i * tall_block, R)
        at = pl.ds(r, tall_block)
        depth = D[at, cols - LANE : width]
        beyond = east(jnp.concatenate([depth, D[at, 0:LANE]], axis=1))[:, : 2 * LANE]
        faces(depth, beyond, FC, WC, at, slice(cols - LANE, width))
        deep = D[pl.ds(r, tall_block + 8), cols:width]
        span = slice(cols, width)
        faces(deep[:tall_block], pltpu.roll(deep, tall_block + 7, 0)[:tall_block], FR, WR, at, span)
        level_terms(deep[:tall_block], at, span)
        return carry

    lax.fori_loop(0, 3, prepare_edge, 0)
    for i in range(5):
        in_copies[i].wait()

    total = wts[0]
    for i in range(1, 16):
        total = total + wts[i]
    one = jnp.ones((1, width), F32)
    scale = one * (-4.0 * coef * wts[c].astype(F32)) / (one * total.astype(F32))

    def south(y):
        return pltpu.roll(y, R + 7, 0)[:R]

    def north(before, y):
        return pltpu.roll(jnp.concatenate([before, y], axis=0), 1, 0)[8:]

    levels, cols_vel, rows_vel = (E, E1, E2, E3), (U, U1, U2, U3), (V, V1, V2, V3)
    cols_sum, rows_sum = (QC, QC1), (QR, QR1)

    def beyond(step, r):
        level = levels[step][pl.ds(r, R), :]
        return east(0.3 * level if step == 0 else level)

    def advance(step, r, ahead):
        here = pl.ds(r, R)
        level = levels[step][pl.ds(r, R + 8), :]
        if step == 0:
            level = 0.3 * level
        wet_c = WC[here, :]
        wet_r = WR[here, :]
        face_c = FC[here, :]
        face_r = FR[here, :]
        mid = level[:R]
        vel_c = (keep * cols_vel[step][here, :] - (ahead - mid) + SX[here, :]) * wet_c
        vel_r = (keep * rows_vel[step][here, :] - (south(level) - mid) + SY[here, :]) * wet_r
        cols_vel[step + 1][here, :] = vel_c
        rows_vel[step + 1][here, :] = vel_r
        flux_c = face_c * vel_c
        flux_r = face_r * vel_r
        level = mid * B[here, :] + A[here, :] - (flux_c - west(flux_c)) - (flux_r - north(CF[step], flux_r))
        if step == 2:
            level = level * (1.0 / 0.3)
        levels[step + 1][here, :] = level
        load_c = vel_c * jnp.abs(vel_c)
        load_r = vel_r * jnp.abs(vel_r)
        if step > 0:
            load_c = load_c + cols_sum[step - 1][here, :]
            load_r = load_r + rows_sum[step - 1][here, :]
        if step < 2:
            cols_sum[step][here, :] = load_c
            rows_sum[step][here, :] = load_r
            CF[step] = flux_r[R - 8 :]
            return
        load_c = wet_c * load_c
        load_r = wet_r * load_r
        T[here, :] = scale * (load_c - west(load_c) + load_r - north(CQ[...], load_r))
        CF[step] = flux_r[R - 8 :]
        CQ[...] = load_r[R - 8 :]

    CF[...] = jnp.zeros((3, 8, width), F32)
    CQ[...] = jnp.zeros((8, width), F32)
    done = [0, 0, 0]

    def sweep(steps, count):
        if count <= 0:
            return
        starts = [done[step] for step in steps]

        def body(i, carry):
            r = pl.multiple_of(i * R, R)
            places = [r + start * R for start in starts]
            ahead = [beyond(step, place) for step, place in zip(steps, places)]
            for step, place, cells in zip(steps, places, ahead):
                advance(step, place, cells)
            return carry

        lax.fori_loop(0, count, body, 0)
        for step in steps:
            done[step] += count

    def run(stop):
        goals = [min(stop + SKEW * (2 - step), nblk) for step in range(3)]
        sweep((0,), min(done[2] + 2 * SKEW, nblk) - done[0])
        sweep((1,), min(done[2] + SKEW, nblk) - done[1])
        sweep((0, 1, 2), goals[0] - done[0])
        sweep((1, 2), goals[1] - done[1])
        sweep((2,), goals[2] - done[2])

    def pack_column():
        rolled = jnp.zeros((8, LANE), F32)
        lane8 = lax.broadcasted_iota(jnp.int32, (8, LANE), 1)
        sub8 = lax.broadcasted_iota(jnp.int32, (8, LANE), 0)

        def take(k, acc):
            cells = T[pl.ds(pl.multiple_of(EDGE + 8 * k, 8), 8), cols:width]
            cells = pltpu.roll(cells, (k + tx) % LANE, 1)
            return jnp.where(lane8 == k, cells, acc)

        rolled = lax.fori_loop(0, rows // 8, take, rolled, unroll=8)
        last = T[nrow - 8 : nrow, 0:LANE]
        T[nrow - 8 : nrow, 0:LANE] = jnp.where(sub8 == 0, last, rolled)
        last = T[nrow - 8 : nrow, LANE : 2 * LANE]
        T[nrow - 8 : nrow, LANE : 2 * LANE] = jnp.where(sub8 == 0, last, pltpu.roll(rolled, 1, 0))

    flying = {}
    sends = []

    def tile(k):
        r0 = sum(chunks[:k]) * R
        return r0, chunks[k] * R // 2

    def each(count, body):
        def loop(i, carry):
            body(pl.multiple_of(i * 8, 8))
            return carry

        lax.fori_loop(0, count // 8, loop, 0)

    def send(k, n, src, dst, peer):
        copy = remote(src, dst, ring_send.at[k, n], ring_recv.at[k, n], peer)
        flying[k, n] = copy
        sends.append(copy)

    def block(j):
        return pl.ds(pl.multiple_of(j * LANE, LANE), LANE)

    def stage0(k):
        r0, h = tile(k)
        h0 = r0 // 2
        theirs = pl.multiple_of(r0 + (1 - core) * h, 8)
        send(k, 0, T.at[pl.ds(theirs, h), 0:cols], CR.at[h0 : h0 + h], sibling)

    def stage1(k):
        r0, h = tile(k)
        h0 = r0 // 2
        mine = pl.multiple_of(r0 + core * h, 8)
        flying[k, 0].wait_recv()

        def body(i):
            at = pl.ds(h0 + i, 8)
            PP[at, :] = T[pl.ds(mine + i, 8), 0:cols] + CR[at, :]

        each(h, body)
        at = pl.ds(h0, h)
        for n, partner in enumerate(partners):
            send(k, 1 + n, PP.at[at, block(parts[n])], RX.at[n, at], partner)

    def stage2(k):
        r0, h = tile(k)
        h0 = r0 // 2
        mine = pl.multiple_of(r0 + core * h, 8)
        for n in range(len(partners)):
            flying[k, 1 + n].wait_recv()

        def body(i):
            at = pl.ds(h0 + i, 8)
            acc = PP[at, block(own_part)]
            for n in range(len(partners)):
                acc = acc + RX[n, at, :]
            M[pl.ds(mine + i, 8), block(own_part)] = acc

        each(h, body)
        own = M.at[pl.ds(mine, h), block(own_part)]
        for n, partner in enumerate(partners):
            send(k, 8 + n, own, own, partner)

    def stage3(k):
        r0, h = tile(k)
        mine = pl.multiple_of(r0 + core * h, 8)
        for n in range(len(partners)):
            flying[k, 8 + n].wait_recv()
        got = M.at[pl.ds(mine, h), 0:cols]
        send(k, 15, got, got, sibling)

    def stage4(k):
        flying[k, 15].wait_recv()

    stages = (stage0, stage1, stage2, stage3, stage4)
    at_stage = [0] * len(chunks)

    def progress(k):
        if at_stage[k] < len(stages):
            stages[at_stage[k]](k)
            at_stage[k] += 1

    for stop, ready in schedule:
        run(stop)
        if stop == nblk:
            pack_column()
        for k in ready:
            progress(k)
    while min(at_stage) < len(stages):
        for k in range(len(chunks)):
            progress(k)

    for copy in halo_copies + strip_copies + sends:
        copy.wait_send()


def finish(rows, cols, E, U, V, BED, M, bn_h, bc_h, hy_h, Z, BN, out_sem):
    nrow = rows + 2 * EDGE
    width = cols + LANE
    ty = lax.axis_index("ty")
    tx = lax.axis_index("tx")
    nty = lax.axis_size("ty")
    ntx = lax.axis_size("tx")
    copies = [
        pltpu.make_async_copy(field.at[EDGE : EDGE + rows, 0:cols], hy_h.at[0, i], out_sem.at[i])
        for i, field in enumerate((E, U, V))
    ]
    copies.append(pltpu.make_async_copy(M.at[EDGE : EDGE + rows, 0:cols], bc_h, out_sem.at[3]))
    for copy in copies:
        copy.start()

    sub8 = lax.broadcasted_iota(jnp.int32, (8, LANE), 0)
    column = jnp.where(sub8 == 0, pltpu.roll(M[nrow - 8 : nrow, LANE : 2 * LANE], 7, 0), M[nrow - 8 : nrow, 0:LANE])

    def spread(k, carry):
        at = pl.ds(pl.multiple_of(EDGE + 8 * k, 8), 8)
        Z[at, :] = pltpu.roll(column, (2 * LANE - k - tx) % LANE, 1)
        return carry

    Z[0:EDGE, :] = jnp.zeros((EDGE, LANE), F32)
    Z[nrow - EDGE : nrow, :] = jnp.zeros((EDGE, LANE), F32)
    lax.fori_loop(0, rows // 8, spread, 0, unroll=8)

    place = lax.broadcasted_iota(jnp.int32, (R, width), 1)
    rows24 = lax.broadcasted_iota(jnp.int32, (R + 8, width), 0)
    inside_c = (place < cols) & (tx * cols + place <= ntx * cols - 2) | (place == width - 1) & (tx > 0)

    def bed_update(i, carry):
        r = pl.multiple_of(EDGE + i * R, 8)
        at = pl.ds(r - 8, R + 16)
        z = BED[at, :] + jnp.concatenate([M[at, :], Z[at, :]], axis=1)
        mid = z[8 : 8 + R]
        slope_c = jnp.where(inside_c, east(mid) - mid, 0.0)
        spill_c = 0.25 * (slope_c - jnp.clip(slope_c, -1.0, 1.0))
        top = z[: R + 8]
        at = rows24 + (ty * rows + i * R - 8)
        below_z = pltpu.roll(z, R + 15, 0)[: R + 8]
        slope_r = jnp.where((at >= 0) & (at <= nty * rows - 2), below_z - top, 0.0)
        spill_r = 0.25 * (slope_r - jnp.clip(slope_r, -1.0, 1.0))
        flow_r = (spill_r - pltpu.roll(spill_r, 1, 0))[8:]
        bed_new = mid + (spill_c - west(spill_c)) + flow_r
        BN[pl.ds(pl.multiple_of(i * R, R), R), :] = bed_new[:, 0:cols]
        return carry

    parts = rows // R // 4
    for part in range(4):
        lax.fori_loop(part * parts, (part + 1) * parts, bed_update, 0)
        at = slice(part * parts * R, (part + 1) * parts * R)
        copies.append(pltpu.make_async_copy(BN.at[at], bn_h.at[at], out_sem.at[4 + part]))
        copies[-1].start()
    for copy in copies:
        copy.wait()


def pinned(ref):
    return ref if PIN else jax.ShapeDtypeStruct(ref.shape, ref.dtype)


def shards(bed, land_mask, cell_class, weights, cond_params, wave_stress, hydro_state):
    rows, cols = bed.shape
    chunks = CHUNKS
    nrow, width = rows + 2 * EDGE, cols + LANE
    assert sum(chunks) * R == nrow
    half = nrow // 2
    vm = pltpu.VMEM
    full = vm((nrow, width), F32)
    tall = vm((nrow + 8, width), F32)
    ints = vm((nrow, width), jnp.int32)
    dma = pltpu.SemaphoreType.DMA
    hbm = pl.BlockSpec(memory_space=pltpu.HBM)
    vmem = pl.BlockSpec(memory_space=pltpu.VMEM)
    merge = pl.pallas_call(
        functools.partial(kernel, rows, cols, chunks, SCHEDULE),
        out_shape=tuple(pinned(ref) for ref in (full, full, full, full, vm((nrow, cols), F32))),
        in_specs=[hbm] * 7,
        out_specs=(vmem,) * 5,
        scratch_shapes=[
            tall, tall, tall, full, full, full, full, full, full, full, full, ints, ints,
            tall, *[full] * 11,
            vm((3, 8, width), F32), vm((8, width), F32),
            vm((6, rows, LANE), F32), vm((2, rows, LANE), jnp.int32),
            vm((rows // GROUPS, LANE), F32), vm((rows // GROUPS + 16, LANE), F32),
            vm((half, cols), F32), vm((half, cols), F32), vm((7, half, LANE), F32),
            pltpu.SMEM((16,), jnp.int32), pltpu.SMEM((1, 4), F32), dma((2,)),
            dma((8,)), dma((8,)), dma((2, 8)), dma((2, 8)), dma((3,)), dma((3,)),
            dma((len(chunks), 16)), dma((len(chunks), 16)),
        ],
        compiler_params=pltpu.CompilerParams(
            collective_id=0, has_side_effects=True, vmem_limit_bytes=MERGE_VMEM
        ),
        name="merge",
    )
    fields = merge(bed, land_mask, cell_class, weights, cond_params, wave_stress, hydro_state)
    if PIN:
        fields = [pltpu.with_memory_space_constraint(field, pltpu.VMEM) for field in fields]
    return pl.pallas_call(
        functools.partial(finish, rows, cols),
        out_shape=(
            jax.ShapeDtypeStruct((rows, cols), F32),
            jax.ShapeDtypeStruct((rows, cols), F32),
            jax.ShapeDtypeStruct(hydro_state.shape, F32),
        ),
        in_specs=[vmem] * 5,
        out_specs=(hbm, hbm, hbm),
        scratch_shapes=[vm((nrow, LANE), F32), vm((rows, cols), F32), dma((8,))],
        compiler_params=pltpu.CompilerParams(vmem_limit_bytes=FINISH_VMEM),
        name="finish",
    )(*fields)


def solution(mesh):
    in_specs = (
        P("ty", "tx"),
        P("ty", "tx"),
        P("ty", "tx"),
        P(),
        P("cond", None),
        P("cond", None, "ty", "tx"),
        P("cond", None, "ty", "tx"),
    )
    out_specs = (P("ty", "tx"), P("ty", "tx"), P("cond", None, "ty", "tx"))
    return jax.shard_map(shards, mesh=mesh, in_specs=in_specs, out_specs=out_specs, check_vma=False)
```

```python
import functools

import jax
import jax.numpy as jnp
from jax import lax
from jax.experimental import pallas as pl
from jax.experimental.pallas import tpu as pltpu
from jax.sharding import PartitionSpec as P

MESH = pl.DeviceIdType.MESH
F32 = jnp.float32
LANE = 128
EDGE = 8
HALO = 4
GROUPS = 4
R = 16
NX = 4
FAR_FIRST = ((1, 2), (1, 1), (1, 3), (0, 2), (1, 0), (0, 1), (0, 3))
SKEW = 2
FR_ROWS = 32
PIN = True
MERGE_VMEM = 56 << 20
FINISH_VMEM = 16 << 20
CHUNKS = (9, 8)
SCHEDULE = ((9, (0,)), (12, (0,)), (17, (1, 1, 0, 1, 0, 1, 0, 1)))


def east(y):
    return pltpu.roll(y, y.shape[1] - 1, 1)


def west(y):
    return pltpu.roll(y, 1, 1)


def kernel(
    rows,
    cols,
    chunks,
    schedule,
    bed_h,
    mask_h,
    cls_h,
    wts_h,
    par_h,
    stress_h,
    hydro_h,
    E3,
    U3,
    V3,
    BED,
    M,
    E,
    E1,
    E2,
    U,
    U1,
    U2,
    V,
    V1,
    V2,
    SX,
    SY,
    MASK,
    CLS,
    D,
    WC,
    WR,
    FC,
    FR,
    A,
    B,
    QC,
    QC1,
    QR,
    QR1,
    T,
    CF,
    CQ,
    EDF,
    EDI,
    PS,
    RSTRIP,
    CR,
    PP,
    RX,
    wts,
    par,
    small_sem,
    row_sem,
    in_sem,
    edge_sem,
    halo_send,
    halo_recv,
    strip_send,
    strip_recv,
    ring_send,
    ring_recv,
):
    nrow = rows + 2 * EDGE
    width = cols + LANE
    nblk = nrow // R
    c = lax.axis_index("cond")
    ty = lax.axis_index("ty")
    tx = lax.axis_index("tx")
    nty = lax.axis_size("ty")
    ntx = lax.axis_size("tx")
    core = c % 2
    x = (c // 2) % NX
    zh = c // (2 * NX)
    up = (ty + nty - 1) % nty
    down = (ty + 1) % nty
    side = 1 - tx

    def cond_of(z, xx, k):
        return (z * NX + xx) * 2 + k

    sibling = (cond_of(zh, x, 1 - core), ty, tx)
    chips = [((zh + dz) % 2, (x + dx) % NX) for dz, dx in FAR_FIRST]
    partners = [(cond_of(z, xx, core), ty, tx) for z, xx in chips]
    parts = [z * NX + xx for z, xx in chips]
    own_part = zh * NX + x
    above = (c, up, tx)
    below = (c, down, tx)
    beside = (c, ty, side)
    diag_up = (c, up, side)
    diag_down = (c, down, side)

    fields = (E, U, V, SX, SY, BED, MASK, CLS)
    sources = (
        hydro_h.at[0, 0],
        hydro_h.at[0, 1],
        hydro_h.at[0, 2],
        stress_h.at[0, 0],
        stress_h.at[0, 1],
        bed_h,
        mask_h,
        cls_h,
    )
    edge_at = pl.multiple_of((1 - tx) * (cols - LANE), LANE)
    edges = [EDF.at[i] for i in range(6)] + [EDI.at[i] for i in range(2)]

    small_copies = [
        pltpu.make_async_copy(wts_h, wts, small_sem.at[0]),
        pltpu.make_async_copy(par_h, par, small_sem.at[1]),
    ]
    for copy in small_copies:
        copy.start()
    edge_copies = [
        pltpu.make_async_copy(src.at[:, pl.ds(edge_at, LANE)], dst, edge_sem.at[i])
        for i, (src, dst) in enumerate(zip(sources, edges))
    ]
    for copy in edge_copies:
        copy.start()
    ends = ((EDGE, 0), (EDGE + rows - 8, rows - 8))
    row_copies = [
        pltpu.make_async_copy(src.at[r : r + 8, :], dst.at[to : to + 8, 0:cols], row_sem.at[n, i])
        for i, (src, dst) in enumerate(zip(sources, fields))
        for n, (to, r) in enumerate(ends)
    ]
    for copy in row_copies:
        copy.start()
    in_copies = [
        pltpu.make_async_copy(src.at[8 : rows - 8, :], dst.at[EDGE + 8 : EDGE + rows - 8, 0:cols], in_sem.at[i])
        for i, (src, dst) in enumerate(zip(sources, fields))
    ]

    barrier = pltpu.get_barrier_semaphore()
    peers = (sibling, *partners, above, below, beside, diag_up, diag_down)
    for peer in peers:
        pl.semaphore_signal(barrier, inc=1, device_id=peer, device_id_type=MESH)
    pad = EDGE - HALO
    for field in fields:
        field[0:pad, 0:cols] = jnp.zeros((pad, cols), field.dtype)
        field[nrow - pad : nrow, 0:cols] = jnp.zeros((pad, cols), field.dtype)
    for level in (E, E1, E2):
        level[nrow : nrow + 8, :] = jnp.zeros((8, width), F32)
    D[nrow : nrow + 8, :] = jnp.zeros((8, width), F32)
    lanes = lax.broadcasted_iota(jnp.int32, (R, LANE), 1)
    for copy in edge_copies + row_copies:
        copy.wait()
    for i in (5, 6, 7, 0, 1, 2, 3, 4):
        in_copies[i].start()

    group = rows // GROUPS

    def pack(i, carry):
        strip = jnp.zeros((R, LANE), F32)
        for g in range(GROUPS):
            r = pl.multiple_of(g * group + i * R, R)
            for k in range(8):
                first = (g * 8 + k) * HALO
                cells = edges[k][pl.ds(r, R), :].astype(F32)
                cells = pltpu.roll(cells, (first + HALO * (1 - tx)) % LANE, 1)
                strip = jnp.where((lanes >= first) & (lanes < first + HALO), cells, strip)
        PS[pl.ds(pl.multiple_of(i * R, R), R), :] = strip
        return carry

    lax.fori_loop(0, group // R, pack, 0)
    pl.semaphore_wait(barrier, len(peers))

    def remote(src, dst, send, recv, peer):
        copy = pltpu.make_async_remote_copy(
            src_ref=src, dst_ref=dst, send_sem=send, recv_sem=recv, device_id=peer, device_id_type=MESH
        )
        copy.start()
        return copy

    halo_copies = []
    for i, dst in enumerate(fields):
        halo_copies.append(
            remote(
                dst.at[EDGE + rows - HALO : EDGE + rows, 0:cols],
                dst.at[EDGE - HALO : EDGE, 0:cols],
                halo_send.at[0, i],
                halo_recv.at[0, i],
                below,
            )
        )
        halo_copies.append(
            remote(
                dst.at[EDGE : EDGE + HALO, 0:cols],
                dst.at[EDGE + rows : EDGE + rows + HALO, 0:cols],
                halo_send.at[1, i],
                halo_recv.at[1, i],
                above,
            )
        )

    strip_copies = [
        remote(PS, RSTRIP.at[8 : 8 + group], strip_send.at[0], strip_recv.at[0], beside),
        remote(PS.at[group - 8 : group], RSTRIP.at[0:8], strip_send.at[1], strip_recv.at[1], diag_down),
        remote(PS.at[0:8], RSTRIP.at[group + 8 : group + 16], strip_send.at[2], strip_recv.at[2], diag_up),
    ]

    def depth_of(mask, bed):
        return mask.astype(F32) * (1.0 + 0.5 * jnp.tanh(-bed))

    in_copies[5].wait()
    in_copies[6].wait()

    def depth_inner(i, carry):
        at = pl.ds(pl.multiple_of(EDGE + i * R, 8), R)
        D[at, 0:cols] = depth_of(MASK[at, 0:cols], BED[at, 0:cols])
        return carry

    lax.fori_loop(0, rows // R, depth_inner, 0)

    for copy in small_copies:
        copy.wait()
    in_copies[7].wait()
    tide = par[0, 0] - 1.0
    fric = 0.2 * par[0, 1]
    coef = par[0, 2]
    flow_in = 0.3 * par[0, 3]
    keep = 1.0 - fric

    def faces(depth, beyond, face, wet, at, span):
        root = jnp.sqrt(depth * beyond)
        wet[at, span] = root / (root + 0.1)
        face[at, span] = 0.3 * root

    def level_terms(depth, at, span):
        kind = CLS[at, span]
        relax = jnp.where(kind == 1, 0.5 * depth, 0.0)
        A[at, span] = 0.3 * (relax * tide + flow_in * jnp.where(kind == 2, depth, 0.0))
        B[at, span] = 1.0 - relax

    def prepare(r, n, span):
        at = pl.ds(r, n)
        deep = D[pl.ds(r, n + 8), span]
        depth = deep[:n]
        faces(depth, east(depth), FC, WC, at, span)
        faces(depth, pltpu.roll(deep, n + 7, 0)[:n], FR, WR, at, span)
        level_terms(depth, at, span)

    def prepare_inner(i, carry):
        prepare(pl.multiple_of(i * R, R), R, slice(0, cols))
        return carry

    lax.fori_loop(1, nblk - 1, prepare_inner, 0)
    for copy in halo_copies:
        copy.wait_recv()
    for copy in strip_copies:
        copy.wait_recv()

    def unpack(n, src, dst, g, real):
        strip = RSTRIP[pl.ds(src, n), :]
        lane = lanes[:n]
        inner = (lane < HALO) & (tx == 0) | (lane >= LANE - HALO) & (tx == 1)
        at = pl.ds(dst, n)
        parts = []
        for k in range(8):
            shift = 2 * LANE - (g * 8 + k) * HALO - HALO * tx
            cells = jnp.where(inner, pltpu.roll(strip, shift % LANE, 1), 0.0)
            parts.append(cells.astype(fields[k].dtype))
            fields[k][at, cols:width] = parts[k]
        depth = depth_of(parts[6], parts[5])
        D[at, cols:width] = depth if real is None else jnp.where(real, depth, 0.0)

    def unpack_rows(i, carry):
        for g in range(GROUPS):
            r = pl.multiple_of(i * R, R)
            unpack(R, 8 + r, pl.multiple_of(EDGE + g * group + r, 8), g, None)
        return carry

    lax.fori_loop(0, group // R, unpack_rows, 0)
    unpack(8, 0, 0, GROUPS - 1, ty > 0)
    unpack(8, group + 8, nrow - 8, 0, ty < nty - 1)
    for r, real in ((0, ty > 0), (nrow - 8, ty < nty - 1)):
        depth = depth_of(MASK[r : r + 8, 0:cols], BED[r : r + 8, 0:cols])
        D[r : r + 8, 0:cols] = jnp.where(real, depth, 0.0)
    for r in (0, nrow - R):
        prepare(r, R, slice(0, width))

    tall_block = (nblk - 2) * R // 3

    def prepare_edge(i, carry):
        r = pl.multiple_of(R + i * tall_block, R)
        at = pl.ds(r, tall_block)
        depth = D[at, cols - LANE : width]
        beyond = east(jnp.concatenate([depth, D[at, 0:LANE]], axis=1))[:, : 2 * LANE]
        faces(depth, beyond, FC, WC, at, slice(cols - LANE, width))
        deep = D[pl.ds(r, tall_block + 8), cols:width]
        span = slice(cols, width)
        faces(deep[:tall_block], pltpu.roll(deep, tall_block + 7, 0)[:tall_block], FR, WR, at, span)
        level_terms(deep[:tall_block], at, span)
        return carry

    lax.fori_loop(0, 3, prepare_edge, 0)
    for i in range(5):
        in_copies[i].wait()

    total = wts[0]
    for i in range(1, 16):
        total = total + wts[i]
    one = jnp.ones((1, width), F32)
    scale = one * (-4.0 * coef * wts[c].astype(F32)) / (one * total.astype(F32))

    def south(y):
        return pltpu.roll(y, R + 7, 0)[:R]

    def north(before, y):
        return pltpu.roll(jnp.concatenate([before, y], axis=0), 1, 0)[8:]

    levels, cols_vel, rows_vel = (E, E1, E2, E3), (U, U1, U2, U3), (V, V1, V2, V3)
    cols_sum, rows_sum = (QC, QC1), (QR, QR1)

    def beyond(step, r):
        level = levels[step][pl.ds(r, R), :]
        return east(0.3 * level if step == 0 else level)

    def advance(step, r, ahead):
        here = pl.ds(r, R)
        level = levels[step][pl.ds(r, R + 8), :]
        if step == 0:
            level = 0.3 * level
        wet_c = WC[here, :]
        wet_r = WR[here, :]
        face_c = FC[here, :]
        face_r = FR[here, :]
        mid = level[:R]
        vel_c = (keep * cols_vel[step][here, :] - (ahead - mid) + SX[here, :]) * wet_c
        vel_r = (keep * rows_vel[step][here, :] - (south(level) - mid) + SY[here, :]) * wet_r
        cols_vel[step + 1][here, :] = vel_c
        rows_vel[step + 1][here, :] = vel_r
        flux_c = face_c * vel_c
        flux_r = face_r * vel_r
        level = mid * B[here, :] + A[here, :] - (flux_c - west(flux_c)) - (flux_r - north(CF[step], flux_r))
        if step == 2:
            level = level * (1.0 / 0.3)
        levels[step + 1][here, :] = level
        load_c = vel_c * jnp.abs(vel_c)
        load_r = vel_r * jnp.abs(vel_r)
        if step > 0:
            load_c = load_c + cols_sum[step - 1][here, :]
            load_r = load_r + rows_sum[step - 1][here, :]
        if step < 2:
            cols_sum[step][here, :] = load_c
            rows_sum[step][here, :] = load_r
            CF[step] = flux_r[R - 8 :]
            return
        load_c = wet_c * load_c
        load_r = wet_r * load_r
        T[here, :] = scale * (load_c - west(load_c) + load_r - north(CQ[...], load_r))
        CF[step] = flux_r[R - 8 :]
        CQ[...] = load_r[R - 8 :]

    CF[...] = jnp.zeros((3, 8, width), F32)
    CQ[...] = jnp.zeros((8, width), F32)
    done = [0, 0, 0]

    def sweep(steps, count):
        if count <= 0:
            return
        starts = [done[step] for step in steps]

        def body(i, carry):
            r = pl.multiple_of(i * R, R)
            places = [r + start * R for start in starts]
            ahead = [beyond(step, place) for step, place in zip(steps, places)]
            for step, place, cells in zip(steps, places, ahead):
                advance(step, place, cells)
            return carry

        lax.fori_loop(0, count, body, 0)
        for step in steps:
            done[step] += count

    def run(stop):
        goals = [min(stop + SKEW * (2 - step), nblk) for step in range(3)]
        sweep((0,), min(done[2] + 2 * SKEW, nblk) - done[0])
        sweep((1,), min(done[2] + SKEW, nblk) - done[1])
        sweep((0, 1, 2), goals[0] - done[0])
        sweep((1, 2), goals[1] - done[1])
        sweep((2,), goals[2] - done[2])

    lane8 = lax.broadcasted_iota(jnp.int32, (8, LANE), 1)
    sub8 = lax.broadcasted_iota(jnp.int32, (8, LANE), 0)

    def pack_column(rolled, first, last):
        def take(k, acc):
            cells = T[pl.ds(pl.multiple_of(EDGE + 8 * k, 8), 8), cols:width]
            cells = pltpu.roll(cells, (k + tx) % LANE, 1)
            return jnp.where(lane8 == k, cells, acc)

        return lax.fori_loop(first, last, take, rolled, unroll=8 if (last - first) % 8 == 0 else 5)

    def place_column(rolled):
        last = T[nrow - 8 : nrow, 0:LANE]
        T[nrow - 8 : nrow, 0:LANE] = jnp.where(sub8 == 0, last, rolled)
        last = T[nrow - 8 : nrow, LANE : 2 * LANE]
        T[nrow - 8 : nrow, LANE : 2 * LANE] = jnp.where(sub8 == 0, last, pltpu.roll(rolled, 1, 0))

    flying = {}
    sends = []

    def tile(k):
        r0 = sum(chunks[:k]) * R
        return r0, chunks[k] * R // 2

    def each(count, body):
        def loop(i, carry):
            body(pl.multiple_of(i * 8, 8))
            return carry

        lax.fori_loop(0, count // 8, loop, 0)

    def send(k, n, src, dst, peer):
        copy = remote(src, dst, ring_send.at[k, n], ring_recv.at[k, n], peer)
        flying[k, n] = copy
        sends.append(copy)

    def block(j):
        return pl.ds(pl.multiple_of(j * LANE, LANE), LANE)

    def stage0(k):
        r0, h = tile(k)
        h0 = r0 // 2
        theirs = pl.multiple_of(r0 + (1 - core) * h, 8)
        send(k, 0, T.at[pl.ds(theirs, h), 0:cols], CR.at[h0 : h0 + h], sibling)

    def stage1(k):
        r0, h = tile(k)
        h0 = r0 // 2
        mine = pl.multiple_of(r0 + core * h, 8)
        flying[k, 0].wait_recv()

        def body(i):
            at = pl.ds(h0 + i, 8)
            PP[at, :] = T[pl.ds(mine + i, 8), 0:cols] + CR[at, :]

        each(h, body)
        at = pl.ds(h0, h)
        for n, partner in enumerate(partners):
            send(k, 1 + n, PP.at[at, block(parts[n])], RX.at[n, at], partner)

    def stage2(k):
        r0, h = tile(k)
        h0 = r0 // 2
        mine = pl.multiple_of(r0 + core * h, 8)
        for n in range(len(partners)):
            flying[k, 1 + n].wait_recv()

        def body(i):
            at = pl.ds(h0 + i, 8)
            acc = PP[at, block(own_part)]
            for n in range(len(partners)):
                acc = acc + RX[n, at, :]
            M[pl.ds(mine + i, 8), block(own_part)] = acc

        each(h, body)
        own = M.at[pl.ds(mine, h), block(own_part)]
        for n, partner in enumerate(partners):
            send(k, 8 + n, own, own, partner)

    def stage3(k):
        r0, h = tile(k)
        mine = pl.multiple_of(r0 + core * h, 8)
        for n in range(len(partners)):
            flying[k, 8 + n].wait_recv()
        got = M.at[pl.ds(mine, h), 0:cols]
        send(k, 15, got, got, sibling)

    def stage4(k):
        flying[k, 15].wait_recv()

    stages = (stage0, stage1, stage2, stage3, stage4)
    at_stage = [0] * len(chunks)

    def progress(k):
        if at_stage[k] < len(stages):
            stages[at_stage[k]](k)
            at_stage[k] += 1

    column, taken = jnp.zeros((8, LANE), F32), 0
    for stop, ready in schedule:
        run(stop)
        if stop < nblk:
            for k in ready:
                progress(k)
        packed = min(stop * R - EDGE, rows) // 8
        column = pack_column(column, taken, packed)
        taken = packed
        if stop == nblk:
            place_column(column)
            for k in ready:
                progress(k)
    while min(at_stage) < len(stages):
        for k in range(len(chunks)):
            progress(k)

    for copy in halo_copies + strip_copies + sends:
        copy.wait_send()


def finish(rows, cols, E, U, V, BED, M, bn_h, bc_h, hy_h, Z, BN, out_sem):
    nrow = rows + 2 * EDGE
    width = cols + LANE
    ty = lax.axis_index("ty")
    tx = lax.axis_index("tx")
    nty = lax.axis_size("ty")
    ntx = lax.axis_size("tx")
    copies = [
        pltpu.make_async_copy(field.at[EDGE : EDGE + rows, 0:cols], hy_h.at[0, i], out_sem.at[i])
        for i, field in enumerate((E, U, V))
    ]
    copies.append(pltpu.make_async_copy(M.at[EDGE : EDGE + rows, 0:cols], bc_h, out_sem.at[3]))
    for copy in copies:
        copy.start()

    sub8 = lax.broadcasted_iota(jnp.int32, (8, LANE), 0)
    column = jnp.where(sub8 == 0, pltpu.roll(M[nrow - 8 : nrow, LANE : 2 * LANE], 7, 0), M[nrow - 8 : nrow, 0:LANE])

    def spread(k, carry):
        at = pl.ds(pl.multiple_of(EDGE + 8 * k, 8), 8)
        Z[at, :] = pltpu.roll(column, (2 * LANE - k - tx) % LANE, 1)
        return carry

    Z[0:EDGE, :] = jnp.zeros((EDGE, LANE), F32)
    Z[nrow - EDGE : nrow, :] = jnp.zeros((EDGE, LANE), F32)
    lax.fori_loop(0, rows // 8, spread, 0, unroll=8)

    place = lax.broadcasted_iota(jnp.int32, (FR_ROWS, width), 1)
    rows24 = lax.broadcasted_iota(jnp.int32, (FR_ROWS + 8, width), 0)
    inside_c = (place < cols) & (tx * cols + place <= ntx * cols - 2) | (place == width - 1) & (tx > 0)

    def bed_update(i, carry):
        r = pl.multiple_of(EDGE + i * FR_ROWS, 8)
        at = pl.ds(r - 8, FR_ROWS + 16)
        z = BED[at, :] + jnp.concatenate([M[at, :], Z[at, :]], axis=1)
        mid = z[8 : 8 + FR_ROWS]
        slope_c = jnp.where(inside_c, east(mid) - mid, 0.0)
        spill_c = 0.25 * (slope_c - jnp.clip(slope_c, -1.0, 1.0))
        top = z[: FR_ROWS + 8]
        at = rows24 + (ty * rows + i * FR_ROWS - 8)
        below_z = pltpu.roll(z, FR_ROWS + 15, 0)[: FR_ROWS + 8]
        slope_r = jnp.where((at >= 0) & (at <= nty * rows - 2), below_z - top, 0.0)
        spill_r = 0.25 * (slope_r - jnp.clip(slope_r, -1.0, 1.0))
        flow_r = (spill_r - pltpu.roll(spill_r, 1, 0))[8:]
        bed_new = mid + (spill_c - west(spill_c)) + flow_r
        BN[pl.ds(pl.multiple_of(i * FR_ROWS, R), FR_ROWS), :] = bed_new[:, 0:cols]
        return carry

    parts = rows // FR_ROWS // 4
    for part in range(4):
        lax.fori_loop(part * parts, (part + 1) * parts, bed_update, 0)
        at = slice(part * parts * FR_ROWS, (part + 1) * parts * FR_ROWS)
        copies.append(pltpu.make_async_copy(BN.at[at], bn_h.at[at], out_sem.at[4 + part]))
        copies[-1].start()
    for copy in copies:
        copy.wait()


def pinned(ref):
    return ref if PIN else jax.ShapeDtypeStruct(ref.shape, ref.dtype)


def shards(bed, land_mask, cell_class, weights, cond_params, wave_stress, hydro_state):
    rows, cols = bed.shape
    chunks = CHUNKS
    nrow, width = rows + 2 * EDGE, cols + LANE
    assert sum(chunks) * R == nrow
    half = nrow // 2
    vm = pltpu.VMEM
    full = vm((nrow, width), F32)
    tall = vm((nrow + 8, width), F32)
    ints = vm((nrow, width), jnp.int32)
    dma = pltpu.SemaphoreType.DMA
    hbm = pl.BlockSpec(memory_space=pltpu.HBM)
    vmem = pl.BlockSpec(memory_space=pltpu.VMEM)
    merge = pl.pallas_call(
        functools.partial(kernel, rows, cols, chunks, SCHEDULE),
        out_shape=tuple(pinned(ref) for ref in (full, full, full, full, vm((nrow, cols), F32))),
        in_specs=[hbm] * 7,
        out_specs=(vmem,) * 5,
        scratch_shapes=[
            tall, tall, tall, full, full, full, full, full, full, full, full, ints, ints,
            tall, *[full] * 11,
            vm((3, 8, width), F32), vm((8, width), F32),
            vm((6, rows, LANE), F32), vm((2, rows, LANE), jnp.int32),
            vm((rows // GROUPS, LANE), F32), vm((rows // GROUPS + 16, LANE), F32),
            vm((half, cols), F32), vm((half, cols), F32), vm((7, half, LANE), F32),
            pltpu.SMEM((16,), jnp.int32), pltpu.SMEM((1, 4), F32), dma((2,)),
            dma((2, 8)), dma((8,)), dma((8,)), dma((2, 8)), dma((2, 8)), dma((3,)), dma((3,)),
            dma((len(chunks), 16)), dma((len(chunks), 16)),
        ],
        compiler_params=pltpu.CompilerParams(
            collective_id=0, has_side_effects=True, vmem_limit_bytes=MERGE_VMEM
        ),
        name="merge",
    )
    fields = merge(bed, land_mask, cell_class, weights, cond_params, wave_stress, hydro_state)
    if PIN:
        fields = [pltpu.with_memory_space_constraint(field, pltpu.VMEM) for field in fields]
    return pl.pallas_call(
        functools.partial(finish, rows, cols),
        out_shape=(
            jax.ShapeDtypeStruct((rows, cols), F32),
            jax.ShapeDtypeStruct((rows, cols), F32),
            jax.ShapeDtypeStruct(hydro_state.shape, F32),
        ),
        in_specs=[vmem] * 5,
        out_specs=(hbm, hbm, hbm),
        scratch_shapes=[vm((nrow, LANE), F32), vm((rows, cols), F32), dma((8,))],
        compiler_params=pltpu.CompilerParams(vmem_limit_bytes=FINISH_VMEM),
        name="finish",
    )(*fields)


def solution(mesh):
    in_specs = (
        P("ty", "tx"),
        P("ty", "tx"),
        P("ty", "tx"),
        P(),
        P("cond", None),
        P("cond", None, "ty", "tx"),
        P("cond", None, "ty", "tx"),
    )
    out_specs = (P("ty", "tx"), P("ty", "tx"), P("cond", None, "ty", "tx"))
    return jax.shard_map(shards, mesh=mesh, in_specs=in_specs, out_specs=out_specs, check_vma=False)
```

```python
import functools

import jax
import jax.numpy as jnp
from jax import lax
from jax.experimental import pallas as pl
from jax.experimental.pallas import tpu as pltpu
from jax.sharding import PartitionSpec as P

MESH = pl.DeviceIdType.MESH
F32 = jnp.float32
LANE = 128
EDGE = 8
HALO = 4
GROUPS = 4
R = 16
NX = 4
FAR_FIRST = ((1, 2), (1, 1), (1, 3), (0, 2), (1, 0), (0, 1), (0, 3))
SKEW = 2
FR_ROWS = 32
PIN = True
MERGE_VMEM = 56 << 20
FINISH_VMEM = 16 << 20
CHUNKS = (9, 8)
SCHEDULE = ((9, (0,)), (12, (0,)), (17, (1, 1, 0, 1, 0, 1, 0, 1)))


def east(y):
    return pltpu.roll(y, y.shape[1] - 1, 1)


def west(y):
    return pltpu.roll(y, 1, 1)


def kernel(
    rows,
    cols,
    chunks,
    schedule,
    bed_h,
    mask_h,
    cls_h,
    wts_h,
    par_h,
    stress_h,
    hydro_h,
    E3,
    U3,
    V3,
    BED,
    M,
    E,
    E1,
    E2,
    U,
    U1,
    U2,
    V,
    V1,
    V2,
    SX,
    SY,
    MASK,
    CLS,
    D,
    WC,
    WR,
    FC,
    FR,
    A,
    B,
    QC,
    QC1,
    QR,
    QR1,
    T,
    CF,
    CQ,
    EDF,
    EDI,
    PS,
    RSTRIP,
    CR,
    PP,
    RX,
    wts,
    par,
    small_sem,
    row_sem,
    in_sem,
    edge_sem,
    halo_send,
    halo_recv,
    strip_send,
    strip_recv,
    ring_send,
    ring_recv,
):
    nrow = rows + 2 * EDGE
    width = cols + LANE
    nblk = nrow // R
    c = lax.axis_index("cond")
    ty = lax.axis_index("ty")
    tx = lax.axis_index("tx")
    nty = lax.axis_size("ty")
    ntx = lax.axis_size("tx")
    core = c % 2
    x = (c // 2) % NX
    zh = c // (2 * NX)
    up = (ty + nty - 1) % nty
    down = (ty + 1) % nty
    side = 1 - tx

    def cond_of(z, xx, k):
        return (z * NX + xx) * 2 + k

    sibling = (cond_of(zh, x, 1 - core), ty, tx)
    chips = [((zh + dz) % 2, (x + dx) % NX) for dz, dx in FAR_FIRST]
    partners = [(cond_of(z, xx, core), ty, tx) for z, xx in chips]
    parts = [z * NX + xx for z, xx in chips]
    own_part = zh * NX + x
    above = (c, up, tx)
    below = (c, down, tx)
    beside = (c, ty, side)
    diag_up = (c, up, side)
    diag_down = (c, down, side)

    fields = (E, U, V, SX, SY, BED, MASK, CLS)
    sources = (
        hydro_h.at[0, 0],
        hydro_h.at[0, 1],
        hydro_h.at[0, 2],
        stress_h.at[0, 0],
        stress_h.at[0, 1],
        bed_h,
        mask_h,
        cls_h,
    )
    edge_at = pl.multiple_of((1 - tx) * (cols - LANE), LANE)
    edges = [EDF.at[i] for i in range(6)] + [EDI.at[i] for i in range(2)]

    small_copies = [
        pltpu.make_async_copy(wts_h, wts, small_sem.at[0]),
        pltpu.make_async_copy(par_h, par, small_sem.at[1]),
    ]
    for copy in small_copies:
        copy.start()
    edge_copies = [
        pltpu.make_async_copy(src.at[:, pl.ds(edge_at, LANE)], dst, edge_sem.at[i])
        for i, (src, dst) in enumerate(zip(sources, edges))
    ]
    for copy in edge_copies:
        copy.start()
    ends = ((EDGE, 0), (EDGE + rows - 8, rows - 8))
    row_copies = [
        pltpu.make_async_copy(src.at[r : r + 8, :], dst.at[to : to + 8, 0:cols], row_sem.at[n, i])
        for i, (src, dst) in enumerate(zip(sources, fields))
        for n, (to, r) in enumerate(ends)
    ]
    for copy in row_copies:
        copy.start()
    in_copies = [
        pltpu.make_async_copy(src.at[8 : rows - 8, :], dst.at[EDGE + 8 : EDGE + rows - 8, 0:cols], in_sem.at[i])
        for i, (src, dst) in enumerate(zip(sources, fields))
    ]

    barrier = pltpu.get_barrier_semaphore()
    peers = (sibling, *partners, above, below, beside, diag_up, diag_down)
    for peer in peers:
        pl.semaphore_signal(barrier, inc=1, device_id=peer, device_id_type=MESH)
    pad = EDGE - HALO
    for field in fields:
        field[0:pad, 0:cols] = jnp.zeros((pad, cols), field.dtype)
        field[nrow - pad : nrow, 0:cols] = jnp.zeros((pad, cols), field.dtype)
    for level in (E, E1, E2):
        level[nrow : nrow + 8, :] = jnp.zeros((8, width), F32)
    D[nrow : nrow + 8, :] = jnp.zeros((8, width), F32)
    lanes = lax.broadcasted_iota(jnp.int32, (R, LANE), 1)
    for copy in edge_copies + row_copies:
        copy.wait()
    for i in (5, 6, 7, 0, 1, 2, 3, 4):
        in_copies[i].start()

    group = rows // GROUPS

    def pack(i, carry):
        strip = jnp.zeros((R, LANE), F32)
        for g in range(GROUPS):
            r = pl.multiple_of(g * group + i * R, R)
            for k in range(8):
                first = (g * 8 + k) * HALO
                cells = edges[k][pl.ds(r, R), :].astype(F32)
                cells = pltpu.roll(cells, (first + HALO * (1 - tx)) % LANE, 1)
                strip = jnp.where((lanes >= first) & (lanes < first + HALO), cells, strip)
        PS[pl.ds(pl.multiple_of(i * R, R), R), :] = strip
        return carry

    lax.fori_loop(0, group // R, pack, 0)
    pl.semaphore_wait(barrier, len(peers))

    def remote(src, dst, send, recv, peer):
        copy = pltpu.make_async_remote_copy(
            src_ref=src, dst_ref=dst, send_sem=send, recv_sem=recv, device_id=peer, device_id_type=MESH
        )
        copy.start()
        return copy

    halo_copies = []
    for i, dst in enumerate(fields):
        halo_copies.append(
            remote(
                dst.at[EDGE + rows - HALO : EDGE + rows, 0:cols],
                dst.at[EDGE - HALO : EDGE, 0:cols],
                halo_send.at[0, i],
                halo_recv.at[0, i],
                below,
            )
        )
        halo_copies.append(
            remote(
                dst.at[EDGE : EDGE + HALO, 0:cols],
                dst.at[EDGE + rows : EDGE + rows + HALO, 0:cols],
                halo_send.at[1, i],
                halo_recv.at[1, i],
                above,
            )
        )

    strip_copies = [
        remote(PS, RSTRIP.at[8 : 8 + group], strip_send.at[0], strip_recv.at[0], beside),
        remote(PS.at[group - 8 : group], RSTRIP.at[0:8], strip_send.at[1], strip_recv.at[1], diag_down),
        remote(PS.at[0:8], RSTRIP.at[group + 8 : group + 16], strip_send.at[2], strip_recv.at[2], diag_up),
    ]

    def depth_of(mask, bed):
        return mask.astype(F32) * (1.0 + 0.5 * jnp.tanh(-bed))

    in_copies[5].wait()
    in_copies[6].wait()

    def depth_inner(i, carry):
        at = pl.ds(pl.multiple_of(EDGE + i * R, 8), R)
        D[at, 0:cols] = depth_of(MASK[at, 0:cols], BED[at, 0:cols])
        return carry

    lax.fori_loop(0, rows // R, depth_inner, 0)

    for copy in small_copies:
        copy.wait()
    in_copies[7].wait()
    tide = par[0, 0] - 1.0
    fric = 0.2 * par[0, 1]
    coef = par[0, 2]
    flow_in = 0.3 * par[0, 3]
    keep = 1.0 - fric

    def faces(depth, beyond, face, wet, at, span):
        root = jnp.sqrt(depth * beyond)
        wet[at, span] = root / (root + 0.1)
        face[at, span] = 0.3 * root

    def level_terms(depth, at, span):
        kind = CLS[at, span]
        relax = jnp.where(kind == 1, 0.5 * depth, 0.0)
        A[at, span] = 0.3 * (relax * tide + flow_in * jnp.where(kind == 2, depth, 0.0))
        B[at, span] = 1.0 - relax

    def prepare(r, n, span):
        at = pl.ds(r, n)
        deep = D[pl.ds(r, n + 8), span]
        depth = deep[:n]
        faces(depth, east(depth), FC, WC, at, span)
        faces(depth, pltpu.roll(deep, n + 7, 0)[:n], FR, WR, at, span)
        level_terms(depth, at, span)

    def prepare_inner(i, carry):
        prepare(pl.multiple_of(i * R, R), R, slice(0, cols))
        return carry

    lax.fori_loop(1, nblk - 1, prepare_inner, 0)
    for copy in halo_copies:
        copy.wait_recv()
    for copy in strip_copies:
        copy.wait_recv()

    def unpack(n, src, dst, g, real):
        strip = RSTRIP[pl.ds(src, n), :]
        lane = lanes[:n]
        inner = (lane < HALO) & (tx == 0) | (lane >= LANE - HALO) & (tx == 1)
        at = pl.ds(dst, n)
        parts = []
        for k in range(8):
            shift = 2 * LANE - (g * 8 + k) * HALO - HALO * tx
            cells = jnp.where(inner, pltpu.roll(strip, shift % LANE, 1), 0.0)
            parts.append(cells.astype(fields[k].dtype))
            fields[k][at, cols:width] = parts[k]
        depth = depth_of(parts[6], parts[5])
        D[at, cols:width] = depth if real is None else jnp.where(real, depth, 0.0)

    def unpack_rows(i, carry):
        for g in range(GROUPS):
            r = pl.multiple_of(i * R, R)
            unpack(R, 8 + r, pl.multiple_of(EDGE + g * group + r, 8), g, None)
        return carry

    lax.fori_loop(0, group // R, unpack_rows, 0)
    unpack(8, 0, 0, GROUPS - 1, ty > 0)
    unpack(8, group + 8, nrow - 8, 0, ty < nty - 1)
    for r, real in ((0, ty > 0), (nrow - 8, ty < nty - 1)):
        depth = depth_of(MASK[r : r + 8, 0:cols], BED[r : r + 8, 0:cols])
        D[r : r + 8, 0:cols] = jnp.where(real, depth, 0.0)
    for r in (0, nrow - R):
        prepare(r, R, slice(0, width))

    tall_block = (nblk - 2) * R // 3

    def prepare_edge(i, carry):
        r = pl.multiple_of(R + i * tall_block, R)
        at = pl.ds(r, tall_block)
        depth = D[at, cols - LANE : width]
        beyond = east(jnp.concatenate([depth, D[at, 0:LANE]], axis=1))[:, : 2 * LANE]
        faces(depth, beyond, FC, WC, at, slice(cols - LANE, width))
        deep = D[pl.ds(r, tall_block + 8), cols:width]
        span = slice(cols, width)
        faces(deep[:tall_block], pltpu.roll(deep, tall_block + 7, 0)[:tall_block], FR, WR, at, span)
        level_terms(deep[:tall_block], at, span)
        return carry

    lax.fori_loop(0, 3, prepare_edge, 0)
    for i in range(5):
        in_copies[i].wait()

    total = wts[0]
    for i in range(1, 16):
        total = total + wts[i]
    one = jnp.ones((1, width), F32)
    scale = one * (-4.0 * coef * wts[c].astype(F32)) / (one * total.astype(F32))

    def south(y):
        return pltpu.roll(y, R + 7, 0)[:R]

    def north(before, y):
        return pltpu.roll(jnp.concatenate([before, y], axis=0), 1, 0)[8:]

    levels, cols_vel, rows_vel = (E, E1, E2, E3), (U, U1, U2, U3), (V, V1, V2, V3)
    cols_sum, rows_sum = (QC, QC1), (QR, QR1)

    def beyond(step, r):
        level = levels[step][pl.ds(r, R), :]
        return east(0.3 * level if step == 0 else level)

    def advance(step, r, ahead):
        here = pl.ds(r, R)
        level = levels[step][pl.ds(r, R + 8), :]
        if step == 0:
            level = 0.3 * level
        wet_c = WC[here, :]
        wet_r = WR[here, :]
        face_c = FC[here, :]
        face_r = FR[here, :]
        mid = level[:R]
        vel_c = (keep * cols_vel[step][here, :] - (ahead - mid) + SX[here, :]) * wet_c
        vel_r = (keep * rows_vel[step][here, :] - (south(level) - mid) + SY[here, :]) * wet_r
        cols_vel[step + 1][here, :] = vel_c
        rows_vel[step + 1][here, :] = vel_r
        flux_c = face_c * vel_c
        flux_r = face_r * vel_r
        level = mid * B[here, :] + A[here, :] - (flux_c - west(flux_c)) - (flux_r - north(CF[step], flux_r))
        if step == 2:
            level = level * (1.0 / 0.3)
        levels[step + 1][here, :] = level
        load_c = vel_c * jnp.abs(vel_c)
        load_r = vel_r * jnp.abs(vel_r)
        if step > 0:
            load_c = load_c + cols_sum[step - 1][here, :]
            load_r = load_r + rows_sum[step - 1][here, :]
        if step < 2:
            cols_sum[step][here, :] = load_c
            rows_sum[step][here, :] = load_r
            CF[step] = flux_r[R - 8 :]
            return
        load_c = wet_c * load_c
        load_r = wet_r * load_r
        T[here, :] = scale * (load_c - west(load_c) + load_r - north(CQ[...], load_r))
        CF[step] = flux_r[R - 8 :]
        CQ[...] = load_r[R - 8 :]

    CF[...] = jnp.zeros((3, 8, width), F32)
    CQ[...] = jnp.zeros((8, width), F32)
    done = [0, 0, 0]

    def sweep(steps, count):
        if count <= 0:
            return
        starts = [done[step] for step in steps]

        def body(i, carry):
            r = pl.multiple_of(i * R, R)
            places = [r + start * R for start in starts]
            ahead = [beyond(step, place) for step, place in zip(steps, places)]
            for step, place, cells in zip(steps, places, ahead):
                advance(step, place, cells)
            return carry

        lax.fori_loop(0, count, body, 0)
        for step in steps:
            done[step] += count

    def run(stop):
        goals = [min(stop + SKEW * (2 - step), nblk) for step in range(3)]
        if not done[0]:
            sweep((0,), SKEW)
            sweep((0, 1), SKEW)
        sweep((0, 1, 2), goals[0] - done[0])
        sweep((1, 2), goals[1] - done[1])
        sweep((2,), goals[2] - done[2])

    lane8 = lax.broadcasted_iota(jnp.int32, (8, LANE), 1)
    sub8 = lax.broadcasted_iota(jnp.int32, (8, LANE), 0)

    def pack_column(rolled, first, last):
        def take(k, acc):
            cells = T[pl.ds(pl.multiple_of(EDGE + 8 * k, 8), 8), cols:width]
            cells = pltpu.roll(cells, (k + tx) % LANE, 1)
            return jnp.where(lane8 == k, cells, acc)

        return lax.fori_loop(first, last, take, rolled, unroll=8 if (last - first) % 8 == 0 else 5)

    def place_column(rolled):
        last = T[nrow - 8 : nrow, 0:LANE]
        T[nrow - 8 : nrow, 0:LANE] = jnp.where(sub8 == 0, last, rolled)
        last = T[nrow - 8 : nrow, LANE : 2 * LANE]
        T[nrow - 8 : nrow, LANE : 2 * LANE] = jnp.where(sub8 == 0, last, pltpu.roll(rolled, 1, 0))

    flying = {}
    sends = []

    def tile(k):
        r0 = sum(chunks[:k]) * R
        return r0, chunks[k] * R // 2

    def each(count, body):
        def loop(i, carry):
            body(pl.multiple_of(i * 8, 8))
            return carry

        lax.fori_loop(0, count // 8, loop, 0)

    def send(k, n, src, dst, peer):
        copy = remote(src, dst, ring_send.at[k, n], ring_recv.at[k, n], peer)
        flying[k, n] = copy
        sends.append(copy)

    def block(j):
        return pl.ds(pl.multiple_of(j * LANE, LANE), LANE)

    def stage0(k):
        r0, h = tile(k)
        h0 = r0 // 2
        theirs = pl.multiple_of(r0 + (1 - core) * h, 8)
        send(k, 0, T.at[pl.ds(theirs, h), 0:cols], CR.at[h0 : h0 + h], sibling)

    def stage1(k):
        r0, h = tile(k)
        h0 = r0 // 2
        mine = pl.multiple_of(r0 + core * h, 8)
        flying[k, 0].wait_recv()

        def body(i):
            at = pl.ds(h0 + i, 8)
            PP[at, :] = T[pl.ds(mine + i, 8), 0:cols] + CR[at, :]

        each(h, body)
        at = pl.ds(h0, h)
        for n, partner in enumerate(partners):
            send(k, 1 + n, PP.at[at, block(parts[n])], RX.at[n, at], partner)

    def stage2(k):
        r0, h = tile(k)
        h0 = r0 // 2
        mine = pl.multiple_of(r0 + core * h, 8)
        for n in range(len(partners)):
            flying[k, 1 + n].wait_recv()

        def body(i):
            at = pl.ds(h0 + i, 8)
            acc = PP[at, block(own_part)]
            for n in range(len(partners)):
                acc = acc + RX[n, at, :]
            M[pl.ds(mine + i, 8), block(own_part)] = acc

        each(h, body)
        own = M.at[pl.ds(mine, h), block(own_part)]
        for n, partner in enumerate(partners):
            send(k, 8 + n, own, own, partner)

    def stage3(k):
        r0, h = tile(k)
        mine = pl.multiple_of(r0 + core * h, 8)
        for n in range(len(partners)):
            flying[k, 8 + n].wait_recv()
        got = M.at[pl.ds(mine, h), 0:cols]
        send(k, 15, got, got, sibling)

    def stage4(k):
        flying[k, 15].wait_recv()

    stages = (stage0, stage1, stage2, stage3, stage4)
    at_stage = [0] * len(chunks)

    def progress(k):
        if at_stage[k] < len(stages):
            stages[at_stage[k]](k)
            at_stage[k] += 1

    column, taken = jnp.zeros((8, LANE), F32), 0
    for stop, ready in schedule:
        run(stop)
        if stop < nblk:
            for k in ready:
                progress(k)
        packed = min(stop * R - EDGE, rows) // 8
        column = pack_column(column, taken, packed)
        taken = packed
        if stop == nblk:
            place_column(column)
            for k in ready:
                progress(k)
    while min(at_stage) < len(stages):
        for k in range(len(chunks)):
            progress(k)

    for copy in halo_copies + strip_copies + sends:
        copy.wait_send()


def finish(rows, cols, E, U, V, BED, M, bn_h, bc_h, hy_h, Z, BN, out_sem):
    nrow = rows + 2 * EDGE
    width = cols + LANE
    ty = lax.axis_index("ty")
    tx = lax.axis_index("tx")
    nty = lax.axis_size("ty")
    ntx = lax.axis_size("tx")
    copies = [
        pltpu.make_async_copy(field.at[EDGE : EDGE + rows, 0:cols], hy_h.at[0, i], out_sem.at[i])
        for i, field in enumerate((E, U, V))
    ]
    copies.append(pltpu.make_async_copy(M.at[EDGE : EDGE + rows, 0:cols], bc_h, out_sem.at[3]))
    for copy in copies:
        copy.start()

    sub8 = lax.broadcasted_iota(jnp.int32, (8, LANE), 0)
    column = jnp.where(sub8 == 0, pltpu.roll(M[nrow - 8 : nrow, LANE : 2 * LANE], 7, 0), M[nrow - 8 : nrow, 0:LANE])

    def spread(k, carry):
        at = pl.ds(pl.multiple_of(EDGE + 8 * k, 8), 8)
        Z[at, :] = pltpu.roll(column, (2 * LANE - k - tx) % LANE, 1)
        return carry

    Z[0:EDGE, :] = jnp.zeros((EDGE, LANE), F32)
    Z[nrow - EDGE : nrow, :] = jnp.zeros((EDGE, LANE), F32)
    lax.fori_loop(0, rows // 8, spread, 0, unroll=8)

    place = lax.broadcasted_iota(jnp.int32, (FR_ROWS, width), 1)
    rows24 = lax.broadcasted_iota(jnp.int32, (FR_ROWS + 8, width), 0)
    inside_c = (place < cols) & (tx * cols + place <= ntx * cols - 2) | (place == width - 1) & (tx > 0)

    def bed_update(i, carry):
        r = pl.multiple_of(EDGE + i * FR_ROWS, 8)
        at = pl.ds(r - 8, FR_ROWS + 16)
        z = BED[at, :] + jnp.concatenate([M[at, :], Z[at, :]], axis=1)
        mid = z[8 : 8 + FR_ROWS]
        slope_c = jnp.where(inside_c, east(mid) - mid, 0.0)
        spill_c = 0.25 * (slope_c - jnp.clip(slope_c, -1.0, 1.0))
        top = z[: FR_ROWS + 8]
        at = rows24 + (ty * rows + i * FR_ROWS - 8)
        below_z = pltpu.roll(z, FR_ROWS + 15, 0)[: FR_ROWS + 8]
        slope_r = jnp.where((at >= 0) & (at <= nty * rows - 2), below_z - top, 0.0)
        spill_r = 0.25 * (slope_r - jnp.clip(slope_r, -1.0, 1.0))
        flow_r = (spill_r - pltpu.roll(spill_r, 1, 0))[8:]
        bed_new = mid + (spill_c - west(spill_c)) + flow_r
        BN[pl.ds(pl.multiple_of(i * FR_ROWS, R), FR_ROWS), :] = bed_new[:, 0:cols]
        return carry

    parts = rows // FR_ROWS // 4
    for part in range(4):
        lax.fori_loop(part * parts, (part + 1) * parts, bed_update, 0)
        at = slice(part * parts * FR_ROWS, (part + 1) * parts * FR_ROWS)
        copies.append(pltpu.make_async_copy(BN.at[at], bn_h.at[at], out_sem.at[4 + part]))
        copies[-1].start()
    for copy in copies:
        copy.wait()


def pinned(ref):
    return ref if PIN else jax.ShapeDtypeStruct(ref.shape, ref.dtype)


def shards(bed, land_mask, cell_class, weights, cond_params, wave_stress, hydro_state):
    rows, cols = bed.shape
    chunks = CHUNKS
    nrow, width = rows + 2 * EDGE, cols + LANE
    assert sum(chunks) * R == nrow
    half = nrow // 2
    vm = pltpu.VMEM
    full = vm((nrow, width), F32)
    tall = vm((nrow + 8, width), F32)
    ints = vm((nrow, width), jnp.int32)
    dma = pltpu.SemaphoreType.DMA
    hbm = pl.BlockSpec(memory_space=pltpu.HBM)
    vmem = pl.BlockSpec(memory_space=pltpu.VMEM)
    merge = pl.pallas_call(
        functools.partial(kernel, rows, cols, chunks, SCHEDULE),
        out_shape=tuple(pinned(ref) for ref in (full, full, full, full, vm((nrow, cols), F32))),
        in_specs=[hbm] * 7,
        out_specs=(vmem,) * 5,
        scratch_shapes=[
            tall, tall, tall, full, full, full, full, full, full, full, full, ints, ints,
            tall, *[full] * 11,
            vm((3, 8, width), F32), vm((8, width), F32),
            vm((6, rows, LANE), F32), vm((2, rows, LANE), jnp.int32),
            vm((rows // GROUPS, LANE), F32), vm((rows // GROUPS + 16, LANE), F32),
            vm((half, cols), F32), vm((half, cols), F32), vm((7, half, LANE), F32),
            pltpu.SMEM((16,), jnp.int32), pltpu.SMEM((1, 4), F32), dma((2,)),
            dma((2, 8)), dma((8,)), dma((8,)), dma((2, 8)), dma((2, 8)), dma((3,)), dma((3,)),
            dma((len(chunks), 16)), dma((len(chunks), 16)),
        ],
        compiler_params=pltpu.CompilerParams(
            collective_id=0, has_side_effects=True, vmem_limit_bytes=MERGE_VMEM
        ),
        name="merge",
    )
    fields = merge(bed, land_mask, cell_class, weights, cond_params, wave_stress, hydro_state)
    if PIN:
        fields = [pltpu.with_memory_space_constraint(field, pltpu.VMEM) for field in fields]
    return pl.pallas_call(
        functools.partial(finish, rows, cols),
        out_shape=(
            jax.ShapeDtypeStruct((rows, cols), F32),
            jax.ShapeDtypeStruct((rows, cols), F32),
            jax.ShapeDtypeStruct(hydro_state.shape, F32),
        ),
        in_specs=[vmem] * 5,
        out_specs=(hbm, hbm, hbm),
        scratch_shapes=[vm((nrow, LANE), F32), vm((rows, cols), F32), dma((8,))],
        compiler_params=pltpu.CompilerParams(vmem_limit_bytes=FINISH_VMEM),
        name="finish",
    )(*fields)


def solution(mesh):
    in_specs = (
        P("ty", "tx"),
        P("ty", "tx"),
        P("ty", "tx"),
        P(),
        P("cond", None),
        P("cond", None, "ty", "tx"),
        P("cond", None, "ty", "tx"),
    )
    out_specs = (P("ty", "tx"), P("ty", "tx"), P("cond", None, "ty", "tx"))
    return jax.shard_map(shards, mesh=mesh, in_specs=in_specs, out_specs=out_specs, check_vma=False)
```
